32 devices in a mesh: gx: 4 (over y, x), gy: 4 (over z), gz: 2 (over core).
Axes of the slice: x: 2, y: 2, z: 4, core: 2. Of those that a mesh axis runs over, the one named last changes fastest.
Arguments:
- pressure: float32 [64, 128, 512], P('gz', 'gx', 'gy'), may hold values from 0.5 to 1.5
- saturation: float32 [64, 128, 512], P('gz', 'gx', 'gy'), may hold values from 0 to 0.5
- dissolved: float32 [64, 128, 512], P('gz', 'gx', 'gy'), may hold values from 0 to 0.12
- old_water: float32 [64, 128, 512], P('gz', 'gx', 'gy'), may hold values from 0.3 to 1
- old_hydrogen: float32 [64, 128, 512], P('gz', 'gx', 'gy'), may hold values from 0 to 0.2
- pore_volume: float32 [64, 128, 512], P('gz', 'gx', 'gy'), may hold values from 1 to 8
- permeability: float32 [64, 128, 512], P('gz', 'gx', 'gy'), may hold values from 0.1 to 10
- frac_pressure: float32 [64, 4096], P('gz', ('gx', 'gy')), may hold values from 0.5 to 1.5
- frac_saturation: float32 [64, 4096], P('gz', ('gx', 'gy')), may hold values from 0 to 0.5
- frac_dissolved: float32 [64, 4096], P('gz', ('gx', 'gy')), may hold values from 0 to 0.12
- frac_old_water: float32 [64, 4096], P('gz', ('gx', 'gy')), may hold values from 0.3 to 1
- frac_old_hydrogen: float32 [64, 4096], P('gz', ('gx', 'gy')), may hold values from 0 to 0.2
- frac_volume: float32 [64, 4096], P('gz', ('gx', 'gy')), may hold values from 0.5 to 4
- pair_segment: int32 [16, 256], P(('gx', 'gy')), may hold values from 0 to 255
- pair_column: int32 [16, 256], P(('gx', 'gy')), may hold values from 0 to 4095
- pair_kind: int32 [16, 256], P(('gx', 'gy')), may hold values from 0 to 63
- pair_count: int32 [16, 16], P(('gx', 'gy')), may hold values from 0 to 16, as said below
- transfer_table: float32 [64], replicated, may hold values from 0.5 to 4
Outputs:
- newton_step: float32 [3, 64, 128, 512], P(None, 'gz', 'gx', 'gy')
- frac_newton_step: float32 [3, 64, 4096], P(None, 'gz', ('gx', 'gy'))
- residual: float32 [3, 64, 128, 512], P(None, 'gz', 'gx', 'gy')
- frac_residual: float32 [3, 64, 4096], P(None, 'gz', ('gx', 'gy'))
The draws below stay inside these ranges and needn't reach their ends.
Inputs may be any that keep to these rules, and one draw needn't show every extreme that they name: `pair_count`: entry [q, o] counts the live pairs between segment block o and column block q; they use slots 0 to that count less one. Some entry equals 16 in every draw.
All inputs are finite; a program needn't handle non-finite values.
Results may differ from the reference program's by a relative error of at most 0.0019.
Values sent between devices are 32-bit elements; how exact they have to be, the bound alone decides.
No kernel may reach another device: no remote copies, remote signals or barrier semaphores. Data moves between devices by JAX's collectives and lax.ppermute only.
A program may use at most 128 MiB of HBM per device.

```python
import math
import jax
import jax.numpy as jnp
from jax import lax

CX = 32
CY = 128
SEG_DEV = 256
CAP = 16
TRANS_KINDS = 64
NZ = 64
NX = 128
NY = 512
BLOCKS_Y = 4
PLANES = 16
SEGMENTS = 4096


def draw_pair_count(key, part):
    counts = jax.random.randint(key, (PLANES, PLANES), 0, CAP + 1, dtype=jnp.int32)
    chosen = jax.random.randint(jax.random.fold_in(key, 11), (), 0, PLANES * PLANES, dtype=jnp.int32)
    flat_index = jnp.arange(PLANES * PLANES, dtype=jnp.int32).reshape(PLANES, PLANES)
    return jnp.where(flat_index == chosen, CAP, counts).astype(jnp.int32)


def place_ends(values, stream_key, low, top_value):
    longest = values.shape.index(max(values.shape))
    spots = []
    for shift in (0, 1):
        where = [jax.random.randint(jax.random.fold_in(stream_key, axis), (), 0, length) for axis, length in enumerate(values.shape)]
        where[longest] = (where[longest] + shift) % values.shape[longest]
        spots.append(tuple(where))
    return values.at[spots[0]].set(low).at[spots[1]].set(top_value)


def shard_levels(key, shape, shards, least, largest):
    loudness, own = 1.0, jax.random.fold_in(key, 6)
    for dim, parts in shards:
        draws = jnp.exp(jax.random.uniform(jax.random.fold_in(own, dim), (parts,), jnp.float32, least / len(shards), largest / len(shards)))
        loudness = loudness * jnp.repeat(draws, shape[dim] // parts).reshape([-1 if axis == dim else 1 for axis in range(len(shape))])
    return loudness


def setup_inputs(seed: int = 0) -> dict:
    seeds = jax.random.split(jax.random.key(seed), 19)
    return {
        "pressure": jnp.clip(0.5 + 1.0 * jax.random.uniform(seeds[0], (NZ, NX, NY), jnp.float32) ** shard_levels(seeds[0], (NZ, NX, NY), ((0, 2), (1, 4), (2, 4)), -0.2, 0.2), 0.5, 1.5),
        "saturation": jnp.clip(0.5 * jax.random.uniform(seeds[1], (NZ, NX, NY), jnp.float32) ** shard_levels(seeds[1], (NZ, NX, NY), ((0, 2), (1, 4), (2, 4)), -0.2, 0.2), 0.0, 0.5),
        "dissolved": jnp.clip(0.12 * jax.random.uniform(seeds[2], (NZ, NX, NY), jnp.float32) ** shard_levels(seeds[2], (NZ, NX, NY), ((0, 2), (1, 4), (2, 4)), -0.2, 0.2), 0.0, 0.12),
        "old_water": jnp.clip(0.3 + 0.7 * jax.random.uniform(seeds[3], (NZ, NX, NY), jnp.float32) ** shard_levels(seeds[3], (NZ, NX, NY), ((0, 2), (1, 4), (2, 4)), -0.2, 0.2), 0.3, 1.0),
        "old_hydrogen": jnp.clip(0.2 * jax.random.uniform(seeds[4], (NZ, NX, NY), jnp.float32) ** shard_levels(seeds[4], (NZ, NX, NY), ((0, 2), (1, 4), (2, 4)), -0.2, 0.2), 0.0, 0.2),
        "pore_volume": jnp.clip(jnp.exp(math.log(8.0) - 2.0794415 * jax.random.uniform(seeds[5], (NZ, NX, NY), jnp.float32) ** shard_levels(seeds[5], (NZ, NX, NY), ((0, 2), (1, 4), (2, 4)), -0.2, 0.2)), 1.0, 8.0),
        "permeability": jnp.clip(jnp.exp(math.log(10.0) - 4.6051702 * jax.random.uniform(seeds[6], (NZ, NX, NY), jnp.float32) ** shard_levels(seeds[6], (NZ, NX, NY), ((0, 2), (1, 4), (2, 4)), -0.2, 0.2)), 0.1, 10.0),
        "frac_pressure": jnp.clip(0.5 + 1.0 * jax.random.uniform(seeds[7], (NZ, SEGMENTS), jnp.float32) ** shard_levels(seeds[7], (NZ, SEGMENTS), ((0, 2), (1, 16)), -0.2, 0.2), 0.5, 1.5),
        "frac_saturation": jnp.clip(0.5 * jax.random.uniform(seeds[8], (NZ, SEGMENTS), jnp.float32) ** shard_levels(seeds[8], (NZ, SEGMENTS), ((0, 2), (1, 16)), -0.2, 0.2), 0.0, 0.5),
        "frac_dissolved": jnp.clip(0.12 * jax.random.uniform(seeds[9], (NZ, SEGMENTS), jnp.float32) ** shard_levels(seeds[9], (NZ, SEGMENTS), ((0, 2), (1, 16)), -0.2, 0.2), 0.0, 0.12),
        "frac_old_water": jnp.clip(0.3 + 0.7 * jax.random.uniform(seeds[10], (NZ, SEGMENTS), jnp.float32) ** shard_levels(seeds[10], (NZ, SEGMENTS), ((0, 2), (1, 16)), -0.2, 0.2), 0.3, 1.0),
        "frac_old_hydrogen": jnp.clip(0.2 * jax.random.uniform(seeds[11], (NZ, SEGMENTS), jnp.float32) ** shard_levels(seeds[11], (NZ, SEGMENTS), ((0, 2), (1, 16)), -0.2, 0.2), 0.0, 0.2),
        "frac_volume": jnp.clip(jnp.exp(math.log(4.0) - 2.0794415 * jax.random.uniform(seeds[12], (NZ, SEGMENTS), jnp.float32) ** shard_levels(seeds[12], (NZ, SEGMENTS), ((0, 2), (1, 16)), -0.2, 0.2)), 0.5, 4.0),
        "pair_segment": place_ends(jax.random.randint(seeds[13], (PLANES, PLANES * CAP), 0, SEG_DEV), jax.random.fold_in(seeds[13], 1), 0, SEG_DEV - 1).astype(jnp.int32),
        "pair_column": place_ends(jax.random.randint(seeds[14], (PLANES, PLANES * CAP), 0, CX * CY), jax.random.fold_in(seeds[14], 1), 0, (CX * CY) - 1).astype(jnp.int32),
        "pair_kind": place_ends(jax.random.randint(seeds[15], (PLANES, PLANES * CAP), 0, TRANS_KINDS), jax.random.fold_in(seeds[15], 1), 0, TRANS_KINDS - 1).astype(jnp.int32),
        "pair_count": draw_pair_count(jax.random.fold_in(seeds[18], 71), 0),
        "transfer_table": jnp.clip(jnp.exp(jax.random.uniform(seeds[17], (TRANS_KINDS,), jnp.float32, math.log(0.5), math.log(4.0))), 0.5, 4.0),
    }


LIQUID_SLOPE = 0.05
GAS_BASE = 0.2
GAS_SLOPE = 0.1
GAS_VISCOSITY = 0.1
SOLUBLE_BASE = 0.05
SOLUBLE_SLOPE = 0.025
SMOOTHING = 0.0001
GRAVITY = 0.5
VERTICAL_RATIO = 0.2
NORM_SHIFT = 1e-06

def phase_terms(pressure, saturation, dissolved):
    liquid_density = 1.0 + LIQUID_SLOPE * pressure
    gas_density = GAS_BASE + GAS_SLOPE * pressure
    liquid_share = (1.0 - saturation) * (1.0 - saturation)
    water_mobility = liquid_density * (1.0 - dissolved) * liquid_share
    solute_mobility = liquid_density * dissolved * liquid_share
    gas_mobility = gas_density * saturation * saturation / GAS_VISCOSITY
    return (water_mobility, solute_mobility, gas_mobility)

def phase_steps(pressure, saturation, dissolved, step_pressure, step_saturation, step_dissolved):
    liquid_density = 1.0 + LIQUID_SLOPE * pressure
    gas_density = GAS_BASE + GAS_SLOPE * pressure
    liquid_share = (1.0 - saturation) * (1.0 - saturation)
    step_density = LIQUID_SLOPE * step_pressure
    step_share = -2.0 * (1.0 - saturation) * step_saturation
    step_water = step_density * (1.0 - dissolved) * liquid_share - liquid_density * step_dissolved * liquid_share + liquid_density * (1.0 - dissolved) * step_share
    step_solute = step_density * dissolved * liquid_share + liquid_density * step_dissolved * liquid_share + liquid_density * dissolved * step_share
    step_gas = (GAS_SLOPE * step_pressure * saturation * saturation + 2.0 * gas_density * saturation * step_saturation) / GAS_VISCOSITY
    return (step_water, step_solute, step_gas)

def phase_masses(pressure, saturation, dissolved):
    liquid_density = 1.0 + LIQUID_SLOPE * pressure
    gas_density = GAS_BASE + GAS_SLOPE * pressure
    water_mass = liquid_density * (1.0 - saturation) * (1.0 - dissolved)
    hydrogen_mass = liquid_density * (1.0 - saturation) * dissolved + gas_density * saturation
    return (water_mass, hydrogen_mass)

def mass_steps(pressure, saturation, dissolved, step_pressure, step_saturation, step_dissolved):
    liquid_density = 1.0 + LIQUID_SLOPE * pressure
    gas_density = GAS_BASE + GAS_SLOPE * pressure
    step_density = LIQUID_SLOPE * step_pressure
    step_water_mass = step_density * (1.0 - saturation) * (1.0 - dissolved) - liquid_density * step_saturation * (1.0 - dissolved) - liquid_density * (1.0 - saturation) * step_dissolved
    step_hydrogen_mass = step_density * (1.0 - saturation) * dissolved - liquid_density * step_saturation * dissolved + liquid_density * (1.0 - saturation) * step_dissolved + GAS_SLOPE * step_pressure * saturation + gas_density * step_saturation
    return (step_water_mass, step_hydrogen_mass)

def closure_residual(pressure, saturation, dissolved):
    solubility_gap = SOLUBLE_BASE + SOLUBLE_SLOPE * pressure - dissolved
    root_value = jnp.sqrt(saturation * saturation + solubility_gap * solubility_gap + SMOOTHING)
    return saturation + solubility_gap - root_value

def closure_step(pressure, saturation, dissolved, step_pressure, step_saturation, step_dissolved):
    solubility_gap = SOLUBLE_BASE + SOLUBLE_SLOPE * pressure - dissolved
    root_value = jnp.sqrt(saturation * saturation + solubility_gap * solubility_gap + SMOOTHING)
    step_gap = SOLUBLE_SLOPE * step_pressure - step_dissolved
    return step_saturation + step_gap - (saturation * step_saturation + solubility_gap * step_gap) / root_value

def face_sides(padded, spatial):
    window = [slice(1, -1), slice(1, -1), slice(1, -1)]
    window[spatial] = slice(0, -1)
    lower_side = padded[tuple(window)]
    window[spatial] = slice(1, None)
    upper_side = padded[tuple(window)]
    return (lower_side, upper_side)

def face_difference(face_flux, spatial):
    extent = face_flux.shape[spatial]
    return lax.slice_in_dim(face_flux, 1, extent, axis=spatial) - lax.slice_in_dim(face_flux, 0, extent - 1, axis=spatial)

def flux_divergence(base_padded, step_padded):
    permeability, pressure, water_mobility, solute_mobility, gas_mobility = base_padded
    water_parts = []
    hydrogen_parts = []
    for spatial in range(3):
        perm_lower, perm_upper = face_sides(permeability, spatial)
        transmit = 2.0 * perm_lower * perm_upper / (perm_lower + perm_upper)
        press_lower, press_upper = face_sides(pressure, spatial)
        liquid_drop = press_lower - press_upper
        gas_drop = press_lower - press_upper
        if spatial == 0:
            transmit = VERTICAL_RATIO * transmit
            mean_pressure = 0.5 * (press_lower + press_upper)
            liquid_drop = liquid_drop + GRAVITY * (1.0 + LIQUID_SLOPE * mean_pressure)
            gas_drop = gas_drop + GRAVITY * (GAS_BASE + GAS_SLOPE * mean_pressure)
        water_lower, water_upper = face_sides(water_mobility, spatial)
        solute_lower, solute_upper = face_sides(solute_mobility, spatial)
        gas_lower, gas_upper = face_sides(gas_mobility, spatial)
        water_mean = 0.5 * (water_lower + water_upper)
        solute_mean = 0.5 * (solute_lower + solute_upper)
        gas_mean = 0.5 * (gas_lower + gas_upper)
        if step_padded is None:
            water_flux = transmit * water_mean * liquid_drop
            hydrogen_flux = transmit * (solute_mean * liquid_drop + gas_mean * gas_drop)
        else:
            step_pressure, step_water, step_solute, step_gas = step_padded
            step_lower, step_upper = face_sides(step_pressure, spatial)
            step_liquid_drop = step_lower - step_upper
            step_gas_drop = step_lower - step_upper
            if spatial == 0:
                step_mean = 0.5 * (step_lower + step_upper)
                step_liquid_drop = step_liquid_drop + GRAVITY * LIQUID_SLOPE * step_mean
                step_gas_drop = step_gas_drop + GRAVITY * GAS_SLOPE * step_mean
            sw_lower, sw_upper = face_sides(step_water, spatial)
            ss_lower, ss_upper = face_sides(step_solute, spatial)
            sg_lower, sg_upper = face_sides(step_gas, spatial)
            water_flux = transmit * (0.5 * (sw_lower + sw_upper) * liquid_drop + water_mean * step_liquid_drop)
            hydrogen_flux = transmit * (0.5 * (ss_lower + ss_upper) * liquid_drop + solute_mean * step_liquid_drop + 0.5 * (sg_lower + sg_upper) * gas_drop + gas_mean * step_gas_drop)
        water_parts.append(face_difference(water_flux, spatial))
        hydrogen_parts.append(face_difference(hydrogen_flux, spatial))
    return (water_parts[0] + water_parts[1] + water_parts[2], hydrogen_parts[0] + hydrogen_parts[1] + hydrogen_parts[2])

def pair_lists(pair_segment, pair_column, pair_kind, pair_count, transfer_table):
    owner_view = pair_segment.reshape(PLANES, PLANES, CAP)
    column_view = jnp.transpose(pair_column.reshape(PLANES, PLANES, CAP), (1, 0, 2))
    kind_view = jnp.transpose(pair_kind.reshape(PLANES, PLANES, CAP), (1, 0, 2))
    count_view = jnp.transpose(pair_count)
    owners = jnp.arange(PLANES, dtype=jnp.int32)[:, None, None]
    peer_index = jnp.arange(PLANES, dtype=jnp.int32)[None, :, None]
    slot_rank = jnp.arange(CAP, dtype=jnp.int32)[None, None, :]
    segment_global = owners * SEG_DEV + owner_view
    cell_x = peer_index // BLOCKS_Y * CX + column_view // CY
    cell_y = peer_index % BLOCKS_Y * CY + column_view % CY
    weight = jnp.where(slot_rank < count_view[:, :, None], transfer_table[kind_view], 0.0)
    return (segment_global.reshape(-1).astype(jnp.int32), cell_x.reshape(-1).astype(jnp.int32), cell_y.reshape(-1).astype(jnp.int32), weight.reshape(-1))

def inner_product(left_pair, right_pair):
    return jnp.sum(left_pair[0] * right_pair[0]) + jnp.sum(left_pair[1] * right_pair[1])

def reference(pressure, saturation, dissolved, old_water, old_hydrogen, pore_volume, permeability, frac_pressure, frac_saturation, frac_dissolved, frac_old_water, frac_old_hydrogen, frac_volume, pair_segment, pair_column, pair_kind, pair_count, transfer_table):
    segment_global, cell_x, cell_y, pair_weight = pair_lists(pair_segment, pair_column, pair_kind, pair_count, transfer_table)
    water_mob, solute_mob, gas_mob = phase_terms(pressure, saturation, dissolved)
    base_padded = tuple((jnp.pad(grid_field, 1) for grid_field in (permeability, pressure, water_mob, solute_mob, gas_mob)))
    water_div, hydrogen_div = flux_divergence(base_padded, None)
    water_mass, hydrogen_mass = phase_masses(pressure, saturation, dissolved)
    frac_water_mob, frac_solute_mob, frac_gas_mob = phase_terms(frac_pressure, frac_saturation, frac_dissolved)
    frac_water_mass, frac_hydrogen_mass = phase_masses(frac_pressure, frac_saturation, frac_dissolved)
    cell_hydrogen_mob = solute_mob + gas_mob
    frac_hydrogen_mob = frac_solute_mob + frac_gas_mob
    cell_rows = (pressure[:, cell_x, cell_y], water_mob[:, cell_x, cell_y], cell_hydrogen_mob[:, cell_x, cell_y])
    frac_rows = (frac_pressure[:, segment_global], frac_water_mob[:, segment_global], frac_hydrogen_mob[:, segment_global])
    pressure_gap = frac_rows[0] - cell_rows[0]
    water_rate = pair_weight * 0.5 * (frac_rows[1] + cell_rows[1]) * pressure_gap
    hydrogen_rate = pair_weight * 0.5 * (frac_rows[2] + cell_rows[2]) * pressure_gap
    matrix_res = jnp.stack([(pore_volume * (water_mass - old_water) + water_div).at[:, cell_x, cell_y].add(-water_rate), (pore_volume * (hydrogen_mass - old_hydrogen) + hydrogen_div).at[:, cell_x, cell_y].add(-hydrogen_rate), closure_residual(pressure, saturation, dissolved)])
    frac_res = jnp.stack([(frac_volume * (frac_water_mass - frac_old_water)).at[:, segment_global].add(water_rate), (frac_volume * (frac_hydrogen_mass - frac_old_hydrogen)).at[:, segment_global].add(hydrogen_rate), closure_residual(frac_pressure, frac_saturation, frac_dissolved)])

    def jacobian(direction):
        step_cells, step_frac = direction
        cell_steps = phase_steps(pressure, saturation, dissolved, step_cells[0], step_cells[1], step_cells[2])
        step_padded = tuple((jnp.pad(grid_field, 1) for grid_field in (step_cells[0], cell_steps[0], cell_steps[1], cell_steps[2])))
        step_water_div, step_hydrogen_div = flux_divergence(base_padded, step_padded)
        step_water_mass, step_hydrogen_mass = mass_steps(pressure, saturation, dissolved, step_cells[0], step_cells[1], step_cells[2])
        frac_steps = phase_steps(frac_pressure, frac_saturation, frac_dissolved, step_frac[0], step_frac[1], step_frac[2])
        frac_mass_steps = mass_steps(frac_pressure, frac_saturation, frac_dissolved, step_frac[0], step_frac[1], step_frac[2])
        cell_step_hydrogen = cell_steps[1] + cell_steps[2]
        frac_step_hydrogen = frac_steps[1] + frac_steps[2]
        step_rows = (step_frac[0][:, segment_global], frac_steps[0][:, segment_global], frac_step_hydrogen[:, segment_global])
        step_cell_rows = (step_cells[0][:, cell_x, cell_y], cell_steps[0][:, cell_x, cell_y], cell_step_hydrogen[:, cell_x, cell_y])
        step_gap = step_rows[0] - step_cell_rows[0]
        step_water_rate = pair_weight * (0.5 * (step_rows[1] + step_cell_rows[1]) * pressure_gap + 0.5 * (frac_rows[1] + cell_rows[1]) * step_gap)
        step_hydrogen_rate = pair_weight * (0.5 * (step_rows[2] + step_cell_rows[2]) * pressure_gap + 0.5 * (frac_rows[2] + cell_rows[2]) * step_gap)
        matrix_image = jnp.stack([(pore_volume * step_water_mass + step_water_div).at[:, cell_x, cell_y].add(-step_water_rate), (pore_volume * step_hydrogen_mass + step_hydrogen_div).at[:, cell_x, cell_y].add(-step_hydrogen_rate), closure_step(pressure, saturation, dissolved, step_cells[0], step_cells[1], step_cells[2])])
        frac_image = jnp.stack([(frac_volume * frac_mass_steps[0]).at[:, segment_global].add(step_water_rate), (frac_volume * frac_mass_steps[1]).at[:, segment_global].add(step_hydrogen_rate), closure_step(frac_pressure, frac_saturation, frac_dissolved, step_frac[0], step_frac[1], step_frac[2])])
        return (matrix_image, frac_image)
    residual_pair = (matrix_res, frac_res)
    initial_norm = jnp.sqrt(inner_product(residual_pair, residual_pair) + NORM_SHIFT)
    first = (-matrix_res / initial_norm, -frac_res / initial_norm)
    image = jacobian(first)
    first_coef = inner_product(image, first)
    left_over = (image[0] - first_coef * first[0], image[1] - first_coef * first[1])
    first_length = jnp.sqrt(inner_product(left_over, left_over) + NORM_SHIFT)
    second = (left_over[0] / first_length, left_over[1] / first_length)
    second_image = jacobian(second)
    coef_one = inner_product(second_image, first)
    coef_two = inner_product(second_image, second)
    remainder = (second_image[0] - coef_one * first[0] - coef_two * second[0], second_image[1] - coef_one * first[1] - coef_two * second[1])
    second_length = jnp.sqrt(inner_product(remainder, remainder) + NORM_SHIFT)
    rotate_norm = jnp.sqrt(first_coef * first_coef + first_length * first_length)
    cosine = first_coef / rotate_norm
    sine_part = first_length / rotate_norm
    upper_coef = cosine * coef_one + sine_part * coef_two
    lower_coef = cosine * coef_two - sine_part * coef_one
    weight_two = -sine_part * initial_norm * lower_coef / (lower_coef * lower_coef + second_length * second_length)
    weight_one = (cosine * initial_norm - upper_coef * weight_two) / rotate_norm
    newton_step = weight_one * first[0] + weight_two * second[0]
    frac_newton_step = weight_one * first[1] + weight_two * second[1]
    return (newton_step, frac_newton_step, matrix_res, frac_res)
```

```python
import functools

import jax
import jax.numpy as jnp
from jax import lax
from jax.experimental import pallas as pl
from jax.experimental.pallas import tpu as pltpu
from jax.sharding import PartitionSpec as P

F32 = jnp.float32
BF16 = jnp.bfloat16
EPS = 1e-06
PLANE = ("gx", "gy")


def swap_slots(mesh_shape):
    slots = []
    for axis in ("gx", "gy", "gz"):
        if mesh_shape[axis] > 1:
            slots.append((axis, 0))
        if mesh_shape[axis] > 2:
            slots.append((axis, 1))
    return tuple(slots)


def swap_pairs(size, odd):
    pairs = []
    for i in range(size):
        up = i % 2 == odd
        partner = (i + 1 if up else i - 1) % size
        pairs.append((i, partner))
    if sorted(j for _, j in pairs) != list(range(size)):
        pairs = [(i, j if abs(i - j) == 1 else i) for i, j in pairs]
    return pairs


def slot_side(axis, odd, sizes):
    index = lax.axis_index(axis)
    high = lax.rem(index, 2) == odd
    valid = jnp.where(high, index + 1 < sizes[axis], index > 0)
    return high, valid


def mobilities(p, s, d):
    share = (1.0 - s) * (1.0 - s)
    scaled = (1.0 + 0.05 * p) * share
    mg = (2.0 + p) * (s * s)
    return scaled * (1.0 - d), scaled * d + mg, mg


def mobility_steps(p, s, d, dp, ds, dd):
    lb = 1.0 + 0.05 * p
    open_s = 1.0 - s
    share = open_s * open_s
    scaled = lb * share
    gas = 2.0 + p
    mg = gas * (s * s)
    step = (0.05 * share) * dp - (2.0 * (lb * open_s)) * ds
    dmg = s * (s * dp + (2.0 * gas) * ds)
    step_d = scaled * dd
    return (
        scaled * (1.0 - d),
        scaled * d + mg,
        mg,
        step * (1.0 - d) - step_d,
        step * d + step_d + dmg,
        dmg,
    )


def masses(p, s, d):
    lb_open = (1.0 + 0.05 * p) * (1.0 - s)
    return lb_open * (1.0 - d), lb_open * d + (0.2 + 0.1 * p) * s


def mass_steps(p, s, d, dp, ds, dd):
    lb = 1.0 + 0.05 * p
    open_s = 1.0 - s
    step = (0.05 * open_s) * dp - lb * ds
    step_d = (lb * open_s) * dd
    return (
        step * (1.0 - d) - step_d,
        step * d + step_d + (0.1 * s) * dp + (0.2 + 0.1 * p) * ds,
    )


def closure(p, s, d):
    gap = 0.05 + 0.025 * p - d
    return s + gap - jnp.sqrt(s * s + gap * gap + 1e-4)


def closure_step(p, s, d, dp, ds, dd):
    gap = 0.05 + 0.025 * p - d
    inverse = lax.rsqrt(s * s + gap * gap + 1e-4)
    dgap = 0.025 * dp - dd
    return ds + dgap - (s * ds + gap * dgap) * inverse


def halves(value):
    high = value.astype(BF16)
    return high, (value - high.astype(F32)).astype(BF16)


def split_dot(value, weights, dims):
    high, low = halves(value)
    dot = functools.partial(
        lax.dot_general, dimension_numbers=(dims, ((), ())), preferred_element_type=F32
    )
    return dot(high, weights) + dot(low, weights)


def one_hot(size, index_row):
    shape = (size, index_row.shape[1])
    rows = lax.broadcasted_iota(jnp.int32, shape, 0)
    return jnp.where(rows == index_row, 1.0, 0.0)


class Plan:
    def __init__(self, mesh_shape, pressure, frac, column, cap):
        self.sizes = dict(mesh_shape)
        self.slots = swap_slots(mesh_shape)
        self.z, self.x, self.y = pressure.shape
        self.seg = frac.shape[1]
        self.pairs = column.shape[1]
        self.peers = self.pairs // cap
        self.cap = cap
        self.rows = self.z * self.x
        self.groups = 128 // cap
        self.pack_rows = 6 * self.z // self.groups
        assert self.y == 128 and self.peers % self.groups == 0


def plane_rows(plan, z):
    return pl.ds(pl.multiple_of(z * plan.x, 8), plan.x)


def gather_cells(plan, fields, column, dst):
    one_y = one_hot(plan.y, lax.rem(column, plan.y)).astype(BF16)
    one_x = one_hot(plan.x, lax.div(column, plan.y))
    step = 8

    def body(c, carry):
        for f, field in enumerate(fields):
            rows = pl.ds(pl.multiple_of(c * step * plan.x, 8), step * plan.x)
            got = split_dot(field[rows, :], one_y, ((1,), (0,)))
            got = got.reshape(step, plan.x, plan.pairs) * one_x[None]
            start = pl.multiple_of((3 + f) * plan.z + c * step, 8)
            dst[pl.ds(start, step), :] = jnp.sum(got, axis=1)
        return carry

    lax.fori_loop(0, plan.z // step, body, 0)


def scatter_cells(plan, rates, column, dsts):
    one_y = one_hot(plan.y, lax.rem(column, plan.y)).astype(BF16)
    one_x = one_hot(plan.x, lax.div(column, plan.y))
    step = 8

    def body(c, carry):
        for f, dst in enumerate(dsts):
            block = rates[pl.ds(pl.multiple_of(f * plan.z + c * step, 8), step), :]
            spread = jnp.concatenate(
                [one_x * block[j : j + 1, :] for j in range(step)], axis=0
            )
            rows = pl.ds(pl.multiple_of(c * step * plan.x, 8), step * plan.x)
            dst[rows, :] = -split_dot(spread, one_y, ((1,), (1,)))
        return carry

    lax.fori_loop(0, plan.z // step, body, 0)


def gather_segments(plan, fields, segment, dst):
    one_s = one_hot(plan.seg, segment).astype(BF16)
    for f, field in enumerate(fields):
        dst[f * plan.z : (f + 1) * plan.z, :] = split_dot(field[...], one_s, ((1,), (0,)))


def scatter_segments(plan, rate, segment):
    one_s = one_hot(plan.seg, segment).astype(BF16)
    return split_dot(rate, one_s, ((1,), (1,)))


def pack_pairs(plan, own, dst):
    n = plan.pack_rows
    lane = lax.broadcasted_iota(jnp.int32, (n, 128), 1) // plan.cap
    for half in range(plan.pairs // 128):
        tiles = [own[g * n : (g + 1) * n, half * 128 : (half + 1) * 128] for g in range(plan.groups)]
        for c in range(plan.groups):
            total = None
            for g in range(plan.groups):
                shift = (g - c) % plan.groups * plan.cap
                moved = pltpu.roll(tiles[g], shift, 1) if shift else tiles[g]
                total = moved if total is None else jnp.where(lane == g, moved, total)
            dst[half * plan.groups + c, 0:n, :] = total


def unpack_pairs(plan, src, dst):
    n = plan.pack_rows
    lane = lax.broadcasted_iota(jnp.int32, (n, 128), 1) // plan.cap
    for half in range(plan.pairs // 128):
        tiles = [src[half * plan.groups + c, 0:n, :] for c in range(plan.groups)]
        for g in range(plan.groups):
            total = None
            for c in range(plan.groups):
                shift = (c - g) % plan.groups * plan.cap
                moved = pltpu.roll(tiles[c], shift, 1) if shift else tiles[c]
                total = moved if total is None else jnp.where(lane == c, moved, total)
            dst[g * n : (g + 1) * n, half * 128 : (half + 1) * 128] = total


def write_faces(plan, fields, outs):
    lane = lax.broadcasted_iota(jnp.int32, (plan.x, 128), 1)
    y_outs = []
    for (axis, odd), out in zip(plan.slots, outs):
        high, _ = slot_side(axis, odd, plan.sizes)
        if axis == "gx":
            row = jnp.where(high, plan.x - 1, 0)
            for f, field in enumerate(fields):
                out[f] = field[pl.ds(row, plan.z, stride=plan.x), :]
        elif axis == "gz":
            start = pl.multiple_of(jnp.where(high, (plan.z - 1) * plan.x, 0), 8)
            for f, field in enumerate(fields):
                out[f] = field[pl.ds(start, plan.x), :]
        else:
            y_outs.append((out, jnp.where(high, 1, 0)))
            out[...] = jnp.zeros(out.shape, F32)
    if not y_outs:
        return

    def body(z, carry):
        for f, field in enumerate(fields):
            value = field[plane_rows(plan, z), :]
            for out, extra in y_outs:
                out[f] = jnp.where(lane == z, pltpu.roll(value, z + extra, 1), out[f])
        return carry

    lax.fori_loop(0, plan.z, body, 0, unroll=4)


def vertical_sign(axis, high):
    if axis != "gz":
        return None
    return jnp.where(high, 1.0, -1.0).astype(F32)


def add_faces(plan, fluxes, dsts, y_store):
    k = 0
    for (axis, odd), pair in zip(plan.slots, fluxes):
        high, _ = slot_side(axis, odd, plan.sizes)
        for dst, flux in zip(dsts, pair):
            if axis == "gx":
                rows = pl.ds(jnp.where(high, plan.x - 1, 0), plan.z, stride=plan.x)
                dst[rows, :] = dst[rows, :] + flux
            elif axis == "gz":
                start = pl.multiple_of(jnp.where(high, (plan.z - 1) * plan.x, 0), 8)
                rows = pl.ds(start, plan.x)
                dst[rows, :] = dst[rows, :] + flux
            else:
                y_store[k] = flux
                k += 1


def y_correction(plan, y_store, z, lane):
    water = hydrogen = None
    k = 0
    for axis, odd in plan.slots:
        if axis != "gy":
            continue
        high, _ = slot_side(axis, odd, plan.sizes)
        target = jnp.where(high, 127, 0)
        shift = lax.rem(target - z + 128, 128)
        parts = [
            jnp.where(lane == target, pltpu.roll(y_store[k + i], shift, 1), 0.0) for i in (0, 1)
        ]
        k += 2
        water = parts[0] if water is None else water + parts[0]
        hydrogen = parts[1] if hydrogen is None else hydrogen + parts[1]
    return water, hydrogen


def divergence(plan, base, steps, conduct, dsts, y_store, fx, fz):
    lane = lax.broadcasted_iota(jnp.int32, (plan.x, 128), 1)
    zero = jnp.zeros((plan.x, 128), F32)
    p_ref, w_ref, h_ref, g_ref = base
    kx, ky, kz = conduct
    for i in (0, 1):
        fz[i] = zero
        fx[i, 0:8, :] = jnp.zeros((8, 128), F32)

    def body(z, carry):
        here = plane_rows(plan, z)
        below = plane_rows(plan, z + 1)
        beside = pl.ds(z * plan.x + 1, plan.x)
        back = lambda v: pltpu.roll(v, 127, 1)
        p0, w0, h0 = p_ref[here, :], w_ref[here, :], h_ref[here, :]
        if steps is not None:
            q0, a0, b0 = steps[0][here, :], steps[1][here, :], steps[2][here, :]

        def flat(conductance, p1, w1, h1, q1=None, a1=None, b1=None):
            drop = p0 - p1
            if steps is None:
                flow = conductance * drop
                return flow * (w0 + w1), flow * (h0 + h1)
            dq = q0 - q1
            return (
                conductance * ((a0 + a1) * drop + (w0 + w1) * dq),
                conductance * ((b0 + b1) * drop + (h0 + h1) * dq),
            )

        fields = (p_ref, w_ref, h_ref) + (() if steps is None else tuple(steps[:3]))
        water, hydrogen = y_correction(plan, y_store, z, lane)
        yw, yh = flat(ky[here, :], *(back(f[here, :]) for f in fields))
        water = water + yw - pltpu.roll(yw, 1, 1)
        hydrogen = hydrogen + yh - pltpu.roll(yh, 1, 1)
        xw, xh = flat(kx[here, :], *(f[beside, :] for f in fields))
        fx[0, 8 : 8 + plan.x, :] = xw
        fx[1, 8 : 8 + plan.x, :] = xh
        water = water + xw - fx[0, 7 : 7 + plan.x, :]
        hydrogen = hydrogen + xh - fx[1, 7 : 7 + plan.x, :]
        p1, w1, h1 = p_ref[below, :], w_ref[below, :], h_ref[below, :]
        g = g_ref[here, :] + g_ref[below, :]
        total = 0.0125 * (p0 + p1)
        drop = p0 - p1 + (0.5 + total)
        extra = total - 0.4
        conductance = kz[here, :]
        if steps is None:
            zw = conductance * ((w0 + w1) * drop)
            zh = conductance * ((h0 + h1) * drop + g * extra)
        else:
            q1, a1, b1 = steps[0][below, :], steps[1][below, :], steps[2][below, :]
            c = steps[3][here, :] + steps[3][below, :]
            dtotal = 0.0125 * (q0 + q1)
            dq = q0 - q1 + dtotal
            zw = conductance * ((a0 + a1) * drop + (w0 + w1) * dq)
            zh = conductance * (
                (b0 + b1) * drop + (h0 + h1) * dq + c * extra + g * dtotal
            )
        dsts[0][here, :] = dsts[0][here, :] + water + zw - fz[0]
        dsts[1][here, :] = dsts[1][here, :] + hydrogen + zh - fz[1]
        fz[0] = zw
        fz[1] = zh
        return carry

    lax.fori_loop(0, plan.z, body, 0)


def clear_tails(plan, refs):
    for ref in refs:
        ref[plan.rows : plan.rows + plan.x + 8, :] = jnp.zeros((plan.x + 8, 128), F32)


def face_flux(sign, conductance, own, other, own_step=None, other_step=None):
    p0, p1 = own[0], other[0]
    if own_step is None:
        (w0, h0, g0), (w1, h1, g1) = mobilities(*own), mobilities(*other)
    else:
        w0, h0, g0, a0, b0, c0 = mobility_steps(*own, *own_step)
        w1, h1, g1, a1, b1, c1 = mobility_steps(*other, *other_step)
        q0, q1 = own_step[0], other_step[0]
    drop = p0 - p1
    if sign is not None:
        total = 0.0125 * (p0 + p1)
        drop = drop + sign * (0.5 + total)
        extra = sign * (total - 0.4)
    if own_step is None:
        water = (w0 + w1) * drop
        hydrogen = (h0 + h1) * drop
        if sign is not None:
            hydrogen = hydrogen + (g0 + g1) * extra
        return conductance * water, conductance * hydrogen
    dq = q0 - q1
    if sign is not None:
        dtotal = sign * (0.0125 * (q0 + q1))
        dq = dq + dtotal
    water = (a0 + a1) * drop + (w0 + w1) * dq
    hydrogen = (b0 + b1) * drop + (h0 + h1) * dq
    if sign is not None:
        hydrogen = hydrogen + (c0 + c1) * extra + (g0 + g1) * dtotal
    return conductance * water, conductance * hydrogen


def first_kernel(plan, *refs):
    n = len(plan.slots)
    p, s, d, k, fp, fs, fd, segment, column, kind, count, table = refs[:12]
    faces, (pack, own, weight) = refs[12 : 12 + n], refs[12 + n :]
    write_faces(plan, (p, s, d, k), faces)
    gather_segments(plan, (fp, fs, fd), segment[...], own)
    gather_cells(plan, (p, s, d), column[...], own)
    pack_pairs(plan, own, pack)
    kinds = kind[...]
    picked = jnp.zeros(kinds.shape, F32)
    for j in range(table.shape[0]):
        picked = jnp.where(kinds == j, table[j], picked)
    slot = lax.broadcasted_iota(jnp.int32, kinds.shape, 1)
    block, rank = slot // plan.cap, lax.rem(slot, plan.cap)
    live = jnp.zeros(kinds.shape, jnp.int32)
    for j in range(plan.peers):
        live = jnp.where(block == j, count[0, j], live)
    picked = jnp.where(rank < live, picked, 0.0)
    weight[...] = picked
    for half in range(plan.pairs // 128):
        tile = jnp.broadcast_to(picked[:, half * 128 : (half + 1) * 128], (8, 128))
        for c in range(plan.groups):
            moved = pltpu.roll(tile, 128 - c * plan.cap, 1) if c else tile
            pack[half * plan.groups + c, plan.pack_rows : plan.pack_rows + 8, :] = moved


def pair_values(plan, ref, side):
    first = 3 * side
    return tuple(ref[(first + f) * plan.z : (first + f + 1) * plan.z, :] for f in range(3))


def residual_kernel(plan, *refs):
    n = len(plan.slots)
    refs = list(refs)
    take = lambda count: [refs.pop(0) for _ in range(count)]
    p, s, d, k, old_water, old_hydrogen, volume = take(7)
    fp, fs, fd, frac_water, frac_hydrogen, frac_volume = take(6)
    segment, column, weight, own, recv = take(5)
    own_faces, recv_faces = take(n), take(n)
    res, frac_res, kx, ky, kz, kb = take(6)
    faces = take(n)
    pack, own_res, got, weight_back = take(4)
    sp, sw, sh, sg, sk, fx, fz, y_store, rates = take(9)
    res_w, res_h, res_c = (res.at[i] for i in range(3))

    unpack_pairs(plan, recv, got)
    lane8 = lax.broadcasted_iota(jnp.int32, (8, 128), 1) // plan.cap
    for half in range(plan.pairs // 128):
        total = None
        for c in range(plan.groups):
            tile = recv[half * plan.groups + c, plan.pack_rows : plan.pack_rows + 8, :]
            moved = pltpu.roll(tile, c * plan.cap, 1) if c else tile
            total = moved if total is None else jnp.where(lane8 == c, moved, total)
        weight_back[:, half * 128 : (half + 1) * 128] = total[0:1, :]

    def pair_rates(weights, seg_values, cell_values):
        w0, h0, _ = mobilities(*seg_values)
        w1, h1, _ = mobilities(*cell_values)
        flow = (0.5 * weights) * (seg_values[0] - cell_values[0])
        return flow * (w0 + w1), flow * (h0 + h1)

    rate_w, rate_h = pair_rates(weight[...], pair_values(plan, got, 0), pair_values(plan, own, 1))
    rates[0 : plan.z, :] = rate_w
    rates[plan.z : 2 * plan.z, :] = rate_h
    scatter_cells(plan, rates, column[...], (res_w, res_h))
    rate_w, rate_h = pair_rates(
        weight_back[...], pair_values(plan, own, 0), pair_values(plan, got, 1)
    )
    fpv, fsv, fdv = fp[...], fs[...], fd[...]
    mass_w, mass_h = masses(fpv, fsv, fdv)
    vol = frac_volume[...]
    frac_res[0] = vol * (mass_w - frac_water[...]) + scatter_segments(plan, rate_w, segment[...])
    frac_res[1] = vol * (mass_h - frac_hydrogen[...]) + scatter_segments(
        plan, rate_h, segment[...]
    )
    frac_res[2] = closure(fpv, fsv, fdv)

    clear_tails(plan, (sp, sw, sh, sg))
    sk[plan.rows : plan.rows + plan.x + 8, :] = jnp.ones((plan.x + 8, 128), F32)
    lane = lax.broadcasted_iota(jnp.int32, (plan.x, 128), 1)
    row = lax.broadcasted_iota(jnp.int32, (plan.x, 128), 0)

    def cells(z, carry):
        here = plane_rows(plan, z)
        pv, sv, dv = p[here, :], s[here, :], d[here, :]
        sp[here, :] = pv
        sw[here, :], sh[here, :], sg[here, :] = mobilities(pv, sv, dv)
        sk[here, :] = k[here, :]
        mw, mh = masses(pv, sv, dv)
        vol = volume[here, :]
        res_w[here, :] = res_w[here, :] + vol * (mw - old_water[here, :])
        res_h[here, :] = res_h[here, :] + vol * (mh - old_hydrogen[here, :])
        res_c[here, :] = closure(pv, sv, dv)
        return carry

    lax.fori_loop(0, plan.z, cells, 0)

    def conductances(z, carry):
        here = plane_rows(plan, z)
        k0 = sk[here, :]
        kx1 = sk[pl.ds(z * plan.x + 1, plan.x), :]
        ky1 = pltpu.roll(k0, 127, 1)
        kz1 = sk[plane_rows(plan, z + 1), :]
        kx[here, :] = jnp.where(row == plan.x - 1, 0.0, k0 * kx1 / (k0 + kx1))
        ky[here, :] = jnp.where(lane == 127, 0.0, k0 * ky1 / (k0 + ky1))
        inner = jnp.where(z == plan.z - 1, 0.0, 0.2).astype(F32)
        kz[here, :] = inner * (k0 * kz1 / (k0 + kz1))
        return carry

    lax.fori_loop(0, plan.z, conductances, 0)

    fluxes = []
    for i, (axis, odd) in enumerate(plan.slots):
        high, valid = slot_side(axis, odd, plan.sizes)
        mine, theirs = own_faces[i], recv_faces[i]
        k0, k1 = mine[3], theirs[3]
        if axis == "gy":
            k0, k1 = jnp.where(lane < plan.z, k0, 1.0), jnp.where(lane < plan.z, k1, 1.0)
        scale = jnp.where(valid, 0.2 if axis == "gz" else 1.0, 0.0).astype(F32)
        conductance = scale * (k0 * k1 / (k0 + k1))
        kb[i] = conductance
        fluxes.append(
            face_flux(
                vertical_sign(axis, high),
                conductance,
                tuple(mine[f] for f in range(3)),
                tuple(theirs[f] for f in range(3)),
            )
        )
    add_faces(plan, fluxes, (res_w, res_h), y_store)
    divergence(plan, (sp, sw, sh, sg), None, (kx, ky, kz), (res_w, res_h), y_store, fx, fz)
    fields = (res_w, res_h, res_c)
    write_faces(plan, fields, faces)
    gather_segments(plan, tuple(frac_res.at[i] for i in range(3)), segment[...], own_res)
    gather_cells(plan, fields, column[...], own_res)
    pack_pairs(plan, own_res, pack)


def total_of(value):
    return jnp.sum(jnp.sum(value, axis=0, keepdims=True), axis=1, keepdims=True)


def block_sums(plan, cell_refs, frac_refs, function, count):
    def body(z, carry):
        here = plane_rows(plan, z)
        for f in range(3):
            parts = function(*(ref[f, here, :] for ref in cell_refs))
            carry = tuple(c + part for c, part in zip(carry, parts))
        return carry

    zero = jnp.zeros((plan.x, 128), F32)
    sums = lax.fori_loop(0, plan.z, body, (zero,) * count, unroll=2)
    sums = [total_of(v) for v in sums]
    for f in range(3):
        parts = function(*(ref[f] for ref in frac_refs))
        sums = [v + total_of(part) for v, part in zip(sums, parts)]
    return sums


def safe_ratio(top, bottom):
    good = bottom > 0.0
    return jnp.where(good, top / jnp.where(good, bottom, 1.0), 0.0)


def jacobian_kernel(plan, last, *refs):
    n = len(plan.slots)
    refs = list(refs)
    take = lambda count: [refs.pop(0) for _ in range(count)]
    p, s, d, volume, kx, ky, kz, kb, vec = take(9)
    fp, fs, fd, frac_volume, frac_vec = take(5)
    segment, column, weight, weight_back, own, got, own_vec, recv = take(8)
    own_faces, recv_faces = take(n), take(n)
    own_vec_faces, recv_vec_faces = take(n), take(n)
    if last:
        base_vec, base_frac, stats_in = take(3)
        out, frac_out, stats = take(3)
    else:
        out, frac_out = take(2)
        faces = take(n)
        pack, own_out, stats = take(3)
    sp, sw, sh, sg, sq, sa, sb, sc, fx, fz, y_store, rates, got_vec = take(13)
    out_w, out_h, out_c = (out.at[i] for i in range(3))

    unpack_pairs(plan, recv, got_vec)

    def pair_rates(weights, seg_values, seg_steps, cell_values, cell_steps):
        w0, h0, _, a0, b0, _ = mobility_steps(*seg_values, *seg_steps)
        w1, h1, _, a1, b1, _ = mobility_steps(*cell_values, *cell_steps)
        drop = seg_values[0] - cell_values[0]
        dq = seg_steps[0] - cell_steps[0]
        half = 0.5 * weights
        return (
            half * ((a0 + a1) * drop + (w0 + w1) * dq),
            half * ((b0 + b1) * drop + (h0 + h1) * dq),
        )

    rate_w, rate_h = pair_rates(
        weight[...],
        pair_values(plan, got, 0),
        pair_values(plan, got_vec, 0),
        pair_values(plan, own, 1),
        pair_values(plan, own_vec, 1),
    )
    rates[0 : plan.z, :] = rate_w
    rates[plan.z : 2 * plan.z, :] = rate_h
    scatter_cells(plan, rates, column[...], (out_w, out_h))
    rate_w, rate_h = pair_rates(
        weight_back[...],
        pair_values(plan, own, 0),
        pair_values(plan, own_vec, 0),
        pair_values(plan, got, 1),
        pair_values(plan, got_vec, 1),
    )
    values = (fp[...], fs[...], fd[...], frac_vec[0], frac_vec[1], frac_vec[2])
    mass_w, mass_h = mass_steps(*values)
    vol = frac_volume[...]
    frac_out[0] = vol * mass_w + scatter_segments(plan, rate_w, segment[...])
    frac_out[1] = vol * mass_h + scatter_segments(plan, rate_h, segment[...])
    frac_out[2] = closure_step(*values)

    clear_tails(plan, (sp, sw, sh, sg, sq, sa, sb, sc))

    def cells(z, carry):
        here = plane_rows(plan, z)
        values = (p[here, :], s[here, :], d[here, :]) + tuple(vec[f, here, :] for f in range(3))
        sp[here, :] = values[0]
        sq[here, :] = values[3]
        moves = mobility_steps(*values)
        for ref, value in zip((sw, sh, sg, sa, sb, sc), moves):
            ref[here, :] = value
        mw, mh = mass_steps(*values)
        vol = volume[here, :]
        out_w[here, :] = out_w[here, :] + vol * mw
        out_h[here, :] = out_h[here, :] + vol * mh
        out_c[here, :] = closure_step(*values)
        return carry

    lax.fori_loop(0, plan.z, cells, 0)
    fluxes = []
    for i, (axis, odd) in enumerate(plan.slots):
        high, _ = slot_side(axis, odd, plan.sizes)
        three = lambda ref: tuple(ref[f] for f in range(3))
        fluxes.append(
            face_flux(
                vertical_sign(axis, high),
                kb[i],
                three(own_faces[i]),
                three(recv_faces[i]),
                three(own_vec_faces[i]),
                three(recv_vec_faces[i]),
            )
        )
    add_faces(plan, fluxes, (out_w, out_h), y_store)
    divergence(
        plan, (sp, sw, sh, sg), (sq, sa, sb, sc), (kx, ky, kz), (out_w, out_h), y_store, fx, fz
    )
    fields = (out_w, out_h, out_c)
    if not last:
        write_faces(plan, fields, faces)
        gather_segments(plan, tuple(frac_out.at[i] for i in range(3)), segment[...], own_out)
        gather_cells(plan, fields, column[...], own_out)
        pack_pairs(plan, own_out, pack)
        rr, rw = block_sums(
            plan, (vec, out), (frac_vec, frac_out), lambda r, w: (r * r, r * w), 2
        )
        share = safe_ratio(rw, rr)
        (uu,) = block_sums(
            plan,
            (vec, out),
            (frac_vec, frac_out),
            lambda r, w: (jnp.square(w - share * r),),
            1,
        )
        r11 = jnp.sqrt(rr)
        found = (r11, safe_ratio(rw, r11), jnp.sqrt(uu), share, uu)
        lane = lax.broadcasted_iota(jnp.int32, (8, 128), 1)
        total = jnp.zeros((8, 128), F32)
        for j, value in enumerate(found):
            total = jnp.where(lane == j, value, total)
        stats[...] = total
        return
    known = stats_in[0:1, :]
    lane1 = lax.broadcasted_iota(jnp.int32, (1, 128), 1)
    r11, r12, r22, share, uu = (
        jnp.sum(jnp.where(lane1 == j, known, 0.0), axis=1, keepdims=True) for j in range(5)
    )
    refs3 = (base_vec, vec, out)
    fracs3 = (base_frac, frac_vec, frac_out)
    rz, uz = block_sums(
        plan, refs3, fracs3, lambda r, w, v: (r * v, (w - share * r) * v), 2
    )
    along_r, along_u = safe_ratio(rz, r11 * r11), safe_ratio(uz, uu)
    (vv,) = block_sums(
        plan,
        refs3,
        fracs3,
        lambda r, w, v: (jnp.square(v - along_r * r - along_u * (w - share * r)),),
        1,
    )
    found = (r11, r12, r22, safe_ratio(rz, r11), safe_ratio(uz, r22), jnp.sqrt(vv))
    lane = lax.broadcasted_iota(jnp.int32, stats.shape, 1)
    total = jnp.zeros(stats.shape, F32)
    for j, value in enumerate(found):
        total = jnp.where(lane == j, value, total)
    stats[...] = total


def step_kernel(plan, stats, res, frac_res, vec, frac_vec, step, frac_step):
    table = stats[...]
    lane = lax.broadcasted_iota(jnp.int32, table.shape, 1)
    r11, r12, r22, r13, r23, r33 = (
        jnp.sum(jnp.where(lane == j, table, 0.0), axis=1, keepdims=True) for j in range(6)
    )
    add = lambda v: jnp.sum(v, axis=0, keepdims=True)
    norm2 = add(r11 * r11) + EPS
    norm = jnp.sqrt(norm2)
    c11 = add(r11 * r12) / norm2
    left1, left2 = r12 - c11 * r11, r22
    c21 = jnp.sqrt(add(left1 * left1 + left2 * left2) / norm2 + EPS)
    scale = 1.0 / (norm * c21)
    second1, second2 = -scale * left1, -scale * left2
    image1 = -scale * (r13 - c11 * r12)
    image2 = -scale * (r23 - c11 * r22)
    image3 = -scale * r33
    first1 = -r11 / norm
    c12 = add(image1 * first1)
    c22 = add(image1 * second1 + image2 * second2)
    u1 = image1 - c12 * first1 - c22 * second1
    u2 = image2 - c22 * second2
    c32_2 = add(u1 * u1 + u2 * u2 + image3 * image3) + EPS
    rho = jnp.sqrt(c11 * c11 + c21 * c21)
    co, si = c11 / rho, c21 / rho
    t1 = co * c12 + si * c22
    t2 = co * c22 - si * c12
    y2 = -si * norm * t2 / (t2 * t2 + c32_2)
    y1 = (co * norm - t1 * y2) / rho
    on_vec = -y2 * scale
    on_res = -y1 / norm - c11 * on_vec

    def body(z, carry):
        here = plane_rows(plan, z)
        for f in range(3):
            step[f, here, :] = on_res * res[f, here, :] + on_vec * vec[f, here, :]
        return carry

    lax.fori_loop(0, plan.z, body, 0, unroll=2)
    for f in range(3):
        frac_step[f] = on_res * frac_res[f] + on_vec * frac_vec[f]


def call(kernel, out_shapes, args, scratch=(), smem=(), flops=0):
    specs = [
        pl.BlockSpec(memory_space=pltpu.SMEM if i in smem else pltpu.VMEM)
        for i in range(len(args))
    ]
    return pl.pallas_call(
        kernel,
        out_shape=[jax.ShapeDtypeStruct(shape, F32) for shape in out_shapes],
        in_specs=specs,
        out_specs=[pl.BlockSpec(memory_space=pltpu.VMEM)] * len(out_shapes),
        scratch_shapes=[pltpu.VMEM(shape, F32) for shape in scratch],
        compiler_params=pltpu.CompilerParams(vmem_limit_bytes=56 << 20),
    )(*args)


def on_device(mesh_shape, *args):
    (
        pressure,
        saturation,
        dissolved,
        old_water,
        old_hydrogen,
        pore_volume,
        permeability,
        frac_pressure,
        frac_saturation,
        frac_dissolved,
        frac_old_water,
        frac_old_hydrogen,
        frac_volume,
        pair_segment,
        pair_column,
        pair_kind,
        pair_count,
        transfer_table,
    ) = args
    cap = pair_column.shape[1] // pair_count.shape[1]
    plan = Plan(mesh_shape, pressure, frac_pressure, pair_column, cap)
    slots = len(plan.slots)
    devices = plan.sizes["gx"] * plan.sizes["gy"] * plan.sizes["gz"]
    flat = lambda a: a.reshape(plan.rows, plan.y)
    p, s, d, k = (flat(a) for a in (pressure, saturation, dissolved, permeability))
    volume = flat(pore_volume)
    field = (plan.rows, plan.y)
    padded = (plan.rows + plan.x + 8, plan.y)
    pair_shape = (6 * plan.z, plan.pairs)
    y_slots = sum(axis == "gy" for axis, _ in plan.slots)
    flux_scratch = [(2, plan.x + 8, plan.y), (2, plan.x, plan.y), (2 * y_slots, plan.x, plan.y)]
    rate_scratch = (2 * plan.z, plan.pairs)

    def exchange(faces, pack):
        got = lax.all_to_all(pack, PLANE, 0, 0, tiled=True)
        moved = [
            lax.ppermute(face, axis, swap_pairs(plan.sizes[axis], odd))
            for (axis, odd), face in zip(plan.slots, faces)
        ]
        return moved, got

    outs = call(
        functools.partial(first_kernel, plan),
        [(4, 32, 128)] * slots
        + [(plan.peers, plan.pack_rows + 8, 128), pair_shape, (1, plan.pairs)],
        [p, s, d, k, frac_pressure, frac_saturation, frac_dissolved]
        + [pair_segment, pair_column, pair_kind, pair_count, transfer_table],
        smem=(10, 11),
    )
    faces, (pack, own, weight) = outs[:slots], outs[slots:]
    recv_faces, recv = exchange(faces, pack)
    outs = call(
        functools.partial(residual_kernel, plan),
        [(3,) + field, (3, plan.z, plan.seg), field, field, field, (slots, 32, 128)]
        + [(3, 32, 128)] * slots
        + [(plan.peers, plan.pack_rows, 128), pair_shape, pair_shape, (1, plan.pairs)],
        [p, s, d, k, flat(old_water), flat(old_hydrogen), volume]
        + [frac_pressure, frac_saturation, frac_dissolved]
        + [frac_old_water, frac_old_hydrogen, frac_volume]
        + [pair_segment, pair_column, weight, own, recv]
        + list(faces)
        + list(recv_faces),
        scratch=[padded] * 5 + flux_scratch + [rate_scratch],
    )
    res, frac_res, kx, ky, kz, kb = outs[:6]
    vec_faces = outs[6 : 6 + slots]
    pack, own_vec, got, weight_back = outs[6 + slots :]

    def image(vec, frac_vec, vec_faces, pack, own_vec, extra):
        recv_vec_faces, recv_vec = exchange(vec_faces, pack)
        last = extra is not None
        shapes = [(3,) + field, (3, plan.z, plan.seg)]
        if last:
            shapes += [(devices, 128)]
        else:
            shapes += [(3, 32, 128)] * slots
            shapes += [(plan.peers, plan.pack_rows, 128), pair_shape, (8, 128)]
        return call(
            functools.partial(jacobian_kernel, plan, last),
            shapes,
            [p, s, d, volume, kx, ky, kz, kb, vec]
            + [frac_pressure, frac_saturation, frac_dissolved, frac_volume, frac_vec]
            + [pair_segment, pair_column, weight, weight_back, own, got, own_vec, recv_vec]
            + list(faces)
            + list(recv_faces)
            + list(vec_faces)
            + list(recv_vec_faces)
            + (list(extra) if last else []),
            scratch=[padded] * 8 + flux_scratch + [rate_scratch, pair_shape],
        )

    outs = image(res, frac_res, vec_faces, pack, own_vec, None)
    vec, frac_vec = outs[:2]
    vec_faces = outs[2 : 2 + slots]
    pack, own_vec, stats = outs[2 + slots :]
    _, _, stats = image(vec, frac_vec, vec_faces, pack, own_vec, (res, frac_res, stats))
    stats = lax.all_to_all(stats, ("gx", "gy", "gz"), 0, 0, tiled=True)
    step, frac_step = call(
        functools.partial(step_kernel, plan),
        [(3,) + field, (3, plan.z, plan.seg)],
        [stats, res, frac_res, vec, frac_vec],
    )
    whole = (3, plan.z, plan.x, plan.y)
    return step.reshape(whole), frac_step, res.reshape(whole), frac_res


def solution(mesh):
    grid = P("gz", "gx", "gy")
    segments = P("gz", PLANE)
    lists = P(PLANE, None)
    return jax.shard_map(
        functools.partial(on_device, dict(mesh.shape)),
        mesh=mesh,
        in_specs=(grid,) * 7 + (segments,) * 6 + (lists,) * 4 + (P(),),
        out_specs=(
            P(None, "gz", "gx", "gy"),
            P(None, "gz", PLANE),
            P(None, "gz", "gx", "gy"),
            P(None, "gz", PLANE),
        ),
        check_vma=False,
    )
```

```python
import functools

import jax
import jax.numpy as jnp
from jax import lax
from jax.experimental import pallas as pl
from jax.experimental.pallas import tpu as pltpu
from jax.sharding import PartitionSpec as P

F32 = jnp.float32
BF16 = jnp.bfloat16
EPS = 1e-06
PLANE = ("gx", "gy")


def swap_slots(mesh_shape):
    slots = []
    for axis in ("gx", "gy", "gz"):
        if mesh_shape[axis] > 1:
            slots.append((axis, 0))
        if mesh_shape[axis] > 2:
            slots.append((axis, 1))
    return tuple(slots)


def swap_pairs(size, odd):
    pairs = []
    for i in range(size):
        up = i % 2 == odd
        partner = (i + 1 if up else i - 1) % size
        pairs.append((i, partner))
    if sorted(j for _, j in pairs) != list(range(size)):
        pairs = [(i, j if abs(i - j) == 1 else i) for i, j in pairs]
    return pairs


def slot_side(axis, odd, sizes):
    index = lax.axis_index(axis)
    high = lax.rem(index, 2) == odd
    valid = jnp.where(high, index + 1 < sizes[axis], index > 0)
    return high, valid


def mobilities(p, s, d):
    share = (1.0 - s) * (1.0 - s)
    scaled = (1.0 + 0.05 * p) * share
    mg = (2.0 + p) * (s * s)
    return scaled * (1.0 - d), scaled * d + mg, mg


def mobility_steps(p, s, d, dp, ds, dd):
    lb = 1.0 + 0.05 * p
    gas = 2.0 + p
    open_s = 1.0 - s
    scaled = lb * (open_s * open_s)
    mg = gas * (s * s)
    solute = scaled * d
    steps = mobility_moves(lb, gas, open_s, s, d, dp, ds, dd)
    return scaled - solute, solute + mg, mg, steps[0], steps[1], steps[2]


def mobility_moves(lb, gas, open_s, s, d, dp, ds, dd):
    by_s = lb * ds
    move = (0.05 * dp) * open_s - by_s
    move_d = (lb * open_s) * dd
    step = open_s * (move - by_s)
    by_p, by_gas = s * dp, gas * ds
    both = by_p + by_gas
    dmg = s * (both + by_gas)
    dml = step * d + open_s * move_d
    return step - dml, dml + dmg, dmg, move, move_d, 0.1 * both


def cell_steps(p, s, d, dp, ds, dd):
    lb = 1.0 + 0.05 * p
    dmw, dmh, dmg, move, move_d, gas_mass = mobility_moves(
        lb, 2.0 + p, 1.0 - s, s, d, dp, ds, dd
    )
    in_liquid = move * d + move_d
    return dmw, dmh, dmg, move - in_liquid, in_liquid + gas_mass, closure_step(p, s, d, dp, ds, dd)


def masses(p, s, d):
    lb_open = (1.0 + 0.05 * p) * (1.0 - s)
    return lb_open * (1.0 - d), lb_open * d + (0.2 + 0.1 * p) * s


def closure(p, s, d):
    gap = 0.05 + 0.025 * p - d
    return s + gap - jnp.sqrt(s * s + gap * gap + 1e-4)


def closure_step(p, s, d, dp, ds, dd):
    gap = 0.05 + 0.025 * p - d
    inverse = lax.rsqrt(s * s + gap * gap + 1e-4)
    dgap = 0.025 * dp - dd
    return ds + dgap - (s * ds + gap * dgap) * inverse


def halves(value):
    high = value.astype(BF16)
    return high, (value - high.astype(F32)).astype(BF16)


def split_dot(value, weights, dims):
    high, low = halves(value)
    dot = functools.partial(
        lax.dot_general, dimension_numbers=(dims, ((), ())), preferred_element_type=F32
    )
    return dot(high, weights) + dot(low, weights)


def one_hot(size, index_row):
    shape = (size, index_row.shape[1])
    rows = lax.broadcasted_iota(jnp.int32, shape, 0)
    return jnp.where(rows == index_row, 1.0, 0.0)


class Plan:
    def __init__(self, mesh_shape, pressure, frac, column, cap):
        self.sizes = dict(mesh_shape)
        self.slots = swap_slots(mesh_shape)
        self.z, self.x, self.y = pressure.shape
        self.seg = frac.shape[1]
        self.pairs = column.shape[1]
        self.peers = self.pairs // cap
        self.cap = cap
        self.rows = self.z * self.x
        self.groups = 128 // cap
        self.pack_rows = 6 * self.z // self.groups
        self.half = self.x // 2
        assert self.y == 128 and self.x == self.z == 32
        assert self.groups == 8 and self.peers % self.groups == 0
        self.faces = []
        for axis, _ in self.slots:
            if axis != "gy" or axis not in self.faces:
                self.faces.append(axis)
        self.slot_face = []
        spot = 0
        for i, (axis, _) in enumerate(self.slots):
            if i and not (axis == "gy" and self.slots[i - 1][0] == "gy"):
                spot += 1
            self.slot_face.append(spot)


def plane_rows(plan, z):
    return pl.ds(pl.multiple_of(z * plan.x, 8), plan.x)


def column_masks(plan, column):
    x, y = lax.div(column, plan.y), lax.rem(column, plan.y)
    wide = one_hot(2 * plan.y, lax.div(x, plan.half) * plan.y + y).astype(BF16)
    return wide, one_hot(plan.half, lax.rem(x, plan.half))


STEP = 8


def gather_cells(plan, fields, column, dst):
    wide, one_x = column_masks(plan, column)

    def body(c, carry):
        for f, field in enumerate(fields):
            rows = pl.ds(pl.multiple_of(c * STEP * plan.x, 8), STEP * plan.x)
            value = field[rows, :].reshape(STEP, plan.x, plan.y)
            sides = [
                value[:, i * plan.half : (i + 1) * plan.half].reshape(STEP * plan.half, plan.y)
                for i in (0, 1)
            ]
            got = split_dot(jnp.concatenate(sides, axis=1), wide, ((1,), (0,)))
            got = got.reshape(STEP, plan.half, plan.pairs) * one_x[None]
            start = pl.multiple_of((3 + f) * plan.z + c * STEP, 8)
            dst[pl.ds(start, STEP), :] = jnp.sum(got, axis=1)
        return carry

    lax.fori_loop(0, plan.z // STEP, body, 0)


def scatter_cells(plan, rates, column, dsts, y_store):
    wide, one_x = column_masks(plan, column)
    lane = lax.broadcasted_iota(jnp.int32, (plan.x, 128), 1)
    edge = (lane == 0) | (lane == 127)

    def body(c, carry):
        for f, dst in enumerate(dsts):
            block = rates[pl.ds(pl.multiple_of(f * plan.z + c * STEP, 8), STEP), :]
            spread = jnp.concatenate(
                [one_x * block[j : j + 1, :] for j in range(STEP)], axis=0
            )
            got = split_dot(spread, wide, ((1,), (1,)))
            for j in range(STEP):
                z = c * STEP + j
                here = plane_rows(plan, z)
                rows = slice(j * plan.half, (j + 1) * plan.half)
                off = jnp.concatenate(
                    [got[rows, i * plan.y : (i + 1) * plan.y] for i in (0, 1)], axis=0
                )
                if "gy" in plan.faces:
                    turn = lax.rem(255 - 2 * z, 128)
                    off = off - jnp.where(edge, pltpu.roll(y_store[f], turn, 1), 0.0)
                dst[here, :] = dst[here, :] - off
        return carry

    lax.fori_loop(0, plan.z // STEP, body, 0)


def gather_segments(plan, fields, segment, dst):
    one_s = one_hot(plan.seg, segment).astype(BF16)
    for f, field in enumerate(fields):
        dst[f * plan.z : (f + 1) * plan.z, :] = split_dot(field[...], one_s, ((1,), (0,)))


def scatter_segments(plan, rate, segment):
    one_s = one_hot(plan.seg, segment).astype(BF16)
    return split_dot(rate, one_s, ((1,), (1,)))


def block_transpose(plan, tiles):
    tiles = list(tiles)
    block = lax.broadcasted_iota(jnp.int32, tiles[0].shape, 1) // plan.cap
    bit = 1
    while bit < plan.groups:
        clear = (block & bit) == 0
        for i in range(plan.groups):
            if i & bit:
                continue
            low, high = tiles[i], tiles[i | bit]
            shift = bit * plan.cap
            tiles[i] = jnp.where(clear, low, pltpu.roll(high, shift, 1))
            tiles[i | bit] = jnp.where(clear, pltpu.roll(low, 128 - shift, 1), high)
        bit *= 2
    return tiles


def pack_pairs(plan, own, dst):
    n = plan.pack_rows
    for half in range(plan.pairs // 128):
        lanes = slice(half * 128, (half + 1) * 128)
        tiles = [own[g * n : (g + 1) * n, lanes] for g in range(plan.groups)]
        for c, tile in enumerate(block_transpose(plan, tiles)):
            dst[half * plan.groups + c, 0:n, :] = tile


def unpack_pairs(plan, src, dst):
    n = plan.pack_rows
    for half in range(plan.pairs // 128):
        lanes = slice(half * 128, (half + 1) * 128)
        tiles = [src[half * plan.groups + c, 0:n, :] for c in range(plan.groups)]
        for g, tile in enumerate(block_transpose(plan, tiles)):
            dst[g * n : (g + 1) * n, lanes] = tile


def write_faces(plan, fields, outs):
    pair = lax.broadcasted_iota(jnp.int32, (plan.x, 128), 1) // 2
    y_out = None
    for (axis, odd), spot in zip(plan.slots, plan.slot_face):
        out = outs[spot]
        high, _ = slot_side(axis, odd, plan.sizes)
        if axis == "gx":
            row = jnp.where(high, plan.x - 1, 0)
            for f, field in enumerate(fields):
                out[f] = field[pl.ds(row, plan.z, stride=plan.x), :]
        elif axis == "gz":
            start = pl.multiple_of(jnp.where(high, (plan.z - 1) * plan.x, 0), 8)
            for f, field in enumerate(fields):
                out[f] = field[pl.ds(start, plan.x), :]
        else:
            y_out = out
    if y_out is None:
        return
    zero = jnp.zeros((plan.x, 128), F32)

    def body(c, carry):
        carry = list(carry)
        for j in range(4):
            z = c * 4 + j
            for f, field in enumerate(fields):
                value = field[plane_rows(plan, z), :]
                carry[f] = jnp.where(pair == z, pltpu.roll(value, 2 * z + 1, 1), carry[f])
        return tuple(carry)

    for f, value in enumerate(lax.fori_loop(0, plan.z // 4, body, (zero,) * len(fields))):
        y_out[f] = value


def merge_faces(plan, own, recv, count):
    lane = lax.broadcasted_iota(jnp.int32, (plan.x, 128), 1)
    even = lane % 2 == 0
    found = []
    y_recv = []
    for i, (axis, odd) in enumerate(plan.slots):
        high, valid = slot_side(axis, odd, plan.sizes)
        mine = tuple(own[plan.slot_face[i]][f] for f in range(count))
        theirs = tuple(recv[i][f] for f in range(count))
        if axis != "gy":
            found.append((axis, high, valid, mine, theirs))
            continue
        y_recv.append((high, theirs))
        if odd or plan.sizes["gy"] == 2:
            first = y_recv[0][0]
            above = tuple(jnp.where(first, a, b) for a, b in zip(y_recv[0][1], y_recv[-1][1]))
            below = tuple(jnp.where(first, b, a) for a, b in zip(y_recv[0][1], y_recv[-1][1]))
            merged = tuple(
                jnp.where(even, pltpu.roll(a, 127, 1), pltpu.roll(b, 1, 1))
                for a, b in zip(above, below)
            )
            index = lax.axis_index("gy")
            up = jnp.where(index + 1 < plan.sizes["gy"], 1, 0)
            down = jnp.where(index > 0, 1, 0)
            inside = jnp.where(even, up, down) * jnp.where(lane < 2 * plan.z, 1, 0)
            found.append((axis, None, inside == 1, mine, merged))
    return found


def vertical_sign(axis, high):
    if axis != "gz":
        return None
    return jnp.where(high, 1.0, -1.0).astype(F32)


def add_faces(plan, faces, fluxes, dsts, y_store):
    for (axis, high, *_), pair in zip(faces, fluxes):
        for i, (dst, flux) in enumerate(zip(dsts, pair)):
            if axis == "gx":
                rows = pl.ds(jnp.where(high, plan.x - 1, 0), plan.z, stride=plan.x)
                dst[rows, :] = dst[rows, :] + flux
            elif axis == "gz":
                start = pl.multiple_of(jnp.where(high, (plan.z - 1) * plan.x, 0), 8)
                rows = pl.ds(start, plan.x)
                dst[rows, :] = dst[rows, :] + flux
            else:
                y_store[i] = flux


UNROLL = 2


def sweep(plan, plane, dsts, fx, carry, first, count):
    def body(c, carry):
        carry = list(carry)
        for u in range(UNROLL):
            z = first + c * UNROLL + u
            here = plane_rows(plan, z)
            for i, (along_y, along_x, along_z) in enumerate(plane(z)):
                slot = 2 * u + i
                total = dsts[i][here, :] + (along_y - pltpu.roll(along_y, 1, 1))
                fx[slot, 8 : 8 + plan.x, :] = along_x
                total = total + (along_x - fx[slot, 7 : 7 + plan.x, :])
                dsts[i][here, :] = total + (along_z - carry[i])
                carry[i] = along_z
        return tuple(carry)

    return lax.fori_loop(0, count // UNROLL, body, carry)


def sweep_start(plan, fx):
    zero = jnp.zeros((plan.x, 128), F32)
    for i in range(2 * UNROLL):
        fx[i, 0:8, :] = jnp.zeros((8, 128), F32)
    return zero, zero


CHUNKS = 4


def chunk_rows(plan, c):
    size = plan.rows // CHUNKS
    return pl.ds(c * size, size)


def chunk_loop(plan, c, body):
    size = plan.z // CHUNKS
    lax.fori_loop(c * size, (c + 1) * size, body, 0)


def residual_plane(plan, base, k_ref, coef):
    p_ref, w_ref, h_ref, g_ref = base
    lane = lax.broadcasted_iota(jnp.int32, (plan.x, 128), 1)
    row = lax.broadcasted_iota(jnp.int32, (plan.x, 128), 0)
    back = lambda v: pltpu.roll(v, 127, 1)

    def plane(z):
        here, below = plane_rows(plan, z), plane_rows(plan, z + 1)
        beside = pl.ds(z * plan.x + 1, plan.x)
        p0, w0, h0, k0 = (r[here, :] for r in (p_ref, w_ref, h_ref, k_ref))
        flows = []
        sides = (
            (0, lane == 127, tuple(back(v) for v in (p0, w0, h0, k0))),
            (3, row == plan.x - 1, tuple(r[beside, :] for r in (p_ref, w_ref, h_ref, k_ref))),
        )
        for spot, last, (p1, w1, h1, k1) in sides:
            k = jnp.where(last, 0.0, k0 * k1 / (k0 + k1))
            drop, w, h = k * (p0 - p1), w0 + w1, h0 + h1
            coef[spot, here, :] = drop
            coef[spot + 1, here, :] = k * w
            coef[spot + 2, here, :] = k * h
            flows.append((drop * w, drop * h))
        p1, w1, h1, k1 = (r[below, :] for r in (p_ref, w_ref, h_ref, k_ref))
        k = jnp.where(z == plan.z - 1, 0.0, 0.2).astype(F32) * (k0 * k1 / (k0 + k1))
        total = 0.0125 * (p0 + p1)
        drop = k * (p0 - p1 + (0.5 + total))
        extra = k * (total - 0.4)
        w, h, g = w0 + w1, h0 + h1, g_ref[here, :] + g_ref[below, :]
        for i, value in enumerate((drop, k * w, k * h, extra, k * g)):
            coef[6 + i, here, :] = value
        flows.append((drop * w, drop * h + extra * g))
        return tuple(zip(*flows))

    return plane


def jacobian_plane(plan, steps, coef):
    q_ref, a_ref, b_ref, c_ref = steps
    back = lambda v: pltpu.roll(v, 127, 1)

    def plane(z):
        here, below = plane_rows(plan, z), plane_rows(plan, z + 1)
        beside = pl.ds(z * plan.x + 1, plan.x)
        q0, a0, b0 = q_ref[here, :], a_ref[here, :], b_ref[here, :]
        flows = []
        sides = (
            (0, tuple(back(v) for v in (q0, a0, b0))),
            (3, tuple(r[beside, :] for r in (q_ref, a_ref, b_ref))),
        )
        for spot, (q1, a1, b1) in sides:
            drop, w, h = (coef[spot + i, here, :] for i in range(3))
            dq = q0 - q1
            flows.append(((a0 + a1) * drop + w * dq, (b0 + b1) * drop + h * dq))
        q1, a1, b1 = q_ref[below, :], a_ref[below, :], b_ref[below, :]
        drop, w, h, extra, g = (coef[6 + i, here, :] for i in range(5))
        dtotal = 0.0125 * (q0 + q1)
        dq = q0 - q1 + dtotal
        c = c_ref[here, :] + c_ref[below, :]
        flows.append(
            ((a0 + a1) * drop + w * dq, (b0 + b1) * drop + h * dq + (c * extra + g * dtotal))
        )
        return tuple(zip(*flows))

    return plane


class Copies:
    def __init__(self, sems):
        self.sems, self.used = sems, 0

    def start(self, src, dst):
        copy = pltpu.make_async_copy(src, dst, self.sems.at[self.used])
        self.used += 1
        copy.start()
        return copy


def wait_all(copies):
    for copy in copies:
        copy.wait()


def clear_tails(plan, refs):
    for ref in refs:
        ref[plan.rows : plan.rows + plan.x + 8, :] = jnp.zeros((plan.x + 8, 128), F32)


def face_flux(sign, conductance, own, other, own_step=None, other_step=None):
    p0, p1 = own[0], other[0]
    if own_step is None:
        (w0, h0, g0), (w1, h1, g1) = mobilities(*own), mobilities(*other)
    else:
        w0, h0, g0, a0, b0, c0 = mobility_steps(*own, *own_step)
        w1, h1, g1, a1, b1, c1 = mobility_steps(*other, *other_step)
        q0, q1 = own_step[0], other_step[0]
    drop = p0 - p1
    if sign is not None:
        total = 0.0125 * (p0 + p1)
        drop = drop + sign * (0.5 + total)
        extra = sign * (total - 0.4)
    if own_step is None:
        water = (w0 + w1) * drop
        hydrogen = (h0 + h1) * drop
        if sign is not None:
            hydrogen = hydrogen + (g0 + g1) * extra
        return conductance * water, conductance * hydrogen
    dq = q0 - q1
    if sign is not None:
        dtotal = sign * (0.0125 * (q0 + q1))
        dq = dq + dtotal
    water = (a0 + a1) * drop + (w0 + w1) * dq
    hydrogen = (b0 + b1) * drop + (h0 + h1) * dq
    if sign is not None:
        hydrogen = hydrogen + (c0 + c1) * extra + (g0 + g1) * dtotal
    return conductance * water, conductance * hydrogen


def first_kernel(plan, *refs):
    n = len(plan.faces)
    grids = refs[:4]
    fp, fs, fd, segment, column, kind, count, table = refs[4:12]
    faces, (pack, own, weight) = refs[12 : 12 + n], refs[12 + n : 15 + n]
    local, sems = refs[15 + n :]
    copies = Copies(sems)
    loads = [copies.start(g, local.at[i]) for i, g in enumerate(grids)]
    gather_segments(plan, (fp, fs, fd), segment[...], own)
    kinds = kind[...]
    picked = jnp.zeros(kinds.shape, F32)
    for j in range(table.shape[0]):
        picked = jnp.where(kinds == j, table[j], picked)
    slot = lax.broadcasted_iota(jnp.int32, kinds.shape, 1)
    block, rank = slot // plan.cap, lax.rem(slot, plan.cap)
    live = jnp.zeros(kinds.shape, jnp.int32)
    for j in range(plan.peers):
        live = jnp.where(block == j, count[0, j], live)
    picked = jnp.where(rank < live, picked, 0.0)
    weight[...] = picked
    for half in range(plan.pairs // 128):
        tile = jnp.broadcast_to(picked[:, half * 128 : (half + 1) * 128], (8, 128))
        for c in range(plan.groups):
            moved = pltpu.roll(tile, 128 - c * plan.cap, 1) if c else tile
            pack[half * plan.groups + c, plan.pack_rows : plan.pack_rows + 8, :] = moved
    wait_all(loads[:3])
    fields = tuple(local.at[i] for i in range(4))
    gather_cells(plan, fields[:3], column[...], own)
    pack_pairs(plan, own, pack)
    wait_all(loads[3:])
    write_faces(plan, fields, faces)


def pair_values(plan, ref, side):
    first = 3 * side
    return tuple(ref[(first + f) * plan.z : (first + f + 1) * plan.z, :] for f in range(3))


def residual_inner(plan, *refs):
    grids, (_, res_out, coef_out) = refs[:7], refs[7:10]
    sp, sk, sw, sh, sg, local, res, coef, fx, sems = refs[10:]
    copies = Copies(sems)
    places = [sp] + [local.at[i] for i in range(5)] + [sk]
    loads = [
        [
            copies.start(grid.at[chunk_rows(plan, c)], place.at[chunk_rows(plan, c)])
            for grid, place in zip(grids, places)
        ]
        for c in range(CHUNKS)
    ]
    s, d, old_water, old_hydrogen, volume = (local.at[i] for i in range(5))
    res_w, res_h, res_c = (res.at[i] for i in range(3))
    clear_tails(plan, (sp, sw, sh, sg))
    sk[plan.rows : plan.rows + plan.x + 8, :] = jnp.ones((plan.x + 8, 128), F32)

    def cells(z, carry):
        here = plane_rows(plan, z)
        pv, sv, dv = sp[here, :], s[here, :], d[here, :]
        sw[here, :], sh[here, :], sg[here, :] = mobilities(pv, sv, dv)
        mw, mh = masses(pv, sv, dv)
        vol = volume[here, :]
        res_w[here, :] = vol * (mw - old_water[here, :])
        res_h[here, :] = vol * (mh - old_hydrogen[here, :])
        res_c[here, :] = closure(pv, sv, dv)
        return carry

    for c in range(CHUNKS):
        wait_all(loads[c])
        chunk_loop(plan, c, cells)
    plane = residual_plane(plan, (sp, sw, sh, sg), sk, coef)
    carry = sweep_start(plan, fx)
    stores = []
    for c in range(CHUNKS):
        size = plan.z // CHUNKS
        carry = sweep(plan, plane, (res_w, res_h), fx, carry, c * size, size)
        rows = chunk_rows(plan, c)
        stores.append(copies.start(res.at[:, rows], res_out.at[:, rows]))
        stores.append(copies.start(coef.at[:, rows], coef_out.at[:, rows]))
    wait_all(stores)


def residual_kernel(plan, *refs):
    n, m = len(plan.slots), len(plan.faces)
    refs = list(refs)
    take = lambda count: [refs.pop(0) for _ in range(count)]
    (res_in,) = take(1)
    fp, fs, fd, frac_water, frac_hydrogen, frac_volume = take(6)
    segment, column, weight, own, recv = take(5)
    own_faces, recv_faces = take(m), take(n)
    res_out, frac_res, kb = take(3)
    faces = take(m)
    pack, own_res, got, weight_back = take(4)
    res, y_store, rates, sems = take(4)
    fields = tuple(res.at[i] for i in range(3))
    copies = Copies(sems)
    load = copies.start(res_in, res)

    unpack_pairs(plan, recv, got)
    lane8 = lax.broadcasted_iota(jnp.int32, (8, 128), 1) // plan.cap
    for half in range(plan.pairs // 128):
        total = None
        for c in range(plan.groups):
            tile = recv[half * plan.groups + c, plan.pack_rows : plan.pack_rows + 8, :]
            moved = pltpu.roll(tile, c * plan.cap, 1) if c else tile
            total = moved if total is None else jnp.where(lane8 == c, moved, total)
        weight_back[:, half * 128 : (half + 1) * 128] = total[0:1, :]

    def pair_rates(weights, seg_values, cell_values):
        w0, h0, _ = mobilities(*seg_values)
        w1, h1, _ = mobilities(*cell_values)
        flow = (0.5 * weights) * (seg_values[0] - cell_values[0])
        return flow * (w0 + w1), flow * (h0 + h1)

    rate_w, rate_h = pair_rates(
        weight_back[...], pair_values(plan, own, 0), pair_values(plan, got, 1)
    )
    fpv, fsv, fdv = fp[...], fs[...], fd[...]
    mass_w, mass_h = masses(fpv, fsv, fdv)
    vol = frac_volume[...]
    frac_res[0] = vol * (mass_w - frac_water[...]) + scatter_segments(plan, rate_w, segment[...])
    frac_res[1] = vol * (mass_h - frac_hydrogen[...]) + scatter_segments(
        plan, rate_h, segment[...]
    )
    frac_res[2] = closure(fpv, fsv, fdv)
    rate_w, rate_h = pair_rates(weight[...], pair_values(plan, got, 0), pair_values(plan, own, 1))
    rates[0 : plan.z, :] = rate_w
    rates[plan.z : 2 * plan.z, :] = rate_h

    found = merge_faces(plan, own_faces, recv_faces, 4)
    fluxes = []
    for i, (axis, high, valid, mine, theirs) in enumerate(found):
        k0, k1 = mine[3], theirs[3]
        scale = 0.2 if axis == "gz" else 1.0
        conductance = jnp.where(
            valid, scale * (k0 * k1 / jnp.where(valid, k0 + k1, 1.0)), 0.0
        )
        kb[i] = conductance
        fluxes.append(face_flux(vertical_sign(axis, high), conductance, mine[:3], theirs[:3]))
    load.wait()
    add_faces(plan, found, fluxes, fields[:2], y_store)
    scatter_cells(plan, rates, column[...], fields[:2], y_store)
    store = copies.start(res, res_out)
    send_parts(plan, fields, frac_res, segment, column, faces, own_res, pack)
    store.wait()


def send_parts(plan, fields, frac_fields, segment, column, faces, own, pack):
    write_faces(plan, fields, faces)
    gather_segments(plan, tuple(frac_fields.at[i] for i in range(3)), segment[...], own)
    gather_cells(plan, fields, column[...], own)
    pack_pairs(plan, own, pack)


def total_of(value):
    return jnp.sum(jnp.sum(value, axis=0, keepdims=True), axis=1, keepdims=True)


def block_sums(plan, cell_refs, frac_refs, function, count):
    def body(z, carry):
        here = plane_rows(plan, z)
        for f in range(3):
            parts = function(*(group[f][here, :] for group in cell_refs))
            carry = tuple(c + part for c, part in zip(carry, parts))
        return carry

    zero = jnp.zeros((plan.x, 128), F32)
    sums = lax.fori_loop(0, plan.z, body, (zero,) * count, unroll=2)
    sums = [total_of(v) for v in sums]
    for f in range(3):
        parts = function(*(ref[f] for ref in frac_refs))
        sums = [v + total_of(part) for v, part in zip(sums, parts)]
    return sums


def safe_ratio(top, bottom):
    good = bottom > 0.0
    return jnp.where(good, top / jnp.where(good, bottom, 1.0), 0.0)


def jacobian_inner(plan, last, *refs):
    refs = list(refs)
    take = lambda count: [refs.pop(0) for _ in range(count)]
    grids = take(4)
    vec_in, coef_in = take(2)
    if last:
        base_in, base_frac, frac_vec = take(3)
        out_back, stats = take(2)
    else:
        (out_back,) = take(1)
    sq, sa, sb, sc, local, coef, out, fx, sems = take(9)
    copies = Copies(sems)
    places = [sq] + [local.at[i] for i in range(6)]
    sources = [vec_in.at[i] for i in range(3)] + list(grids)
    loads = [
        [
            copies.start(grid.at[chunk_rows(plan, c)], place.at[chunk_rows(plan, c)])
            for grid, place in zip(sources, places)
        ]
        for c in range(CHUNKS)
    ]
    coefs = [
        copies.start(coef_in.at[:, chunk_rows(plan, c)], coef.at[:, chunk_rows(plan, c)])
        for c in range(CHUNKS)
    ]
    if last:
        (base,) = take(1)
        late = copies.start(base_in, base)
    v1, v2, p, s, d, volume = (local.at[i] for i in range(6))
    out_w, out_h, out_c = (out.at[i] for i in range(3))
    clear_tails(plan, (sq, sa, sb, sc))

    def cells(z, carry):
        here = plane_rows(plan, z)
        values = tuple(r[here, :] for r in (p, s, d, sq, v1, v2))
        sa[here, :], sb[here, :], sc[here, :], mw, mh, out_c[here, :] = cell_steps(*values)
        vol = volume[here, :]
        out_w[here, :] = vol * mw
        out_h[here, :] = vol * mh
        return carry

    for c in range(CHUNKS):
        wait_all(loads[c])
        chunk_loop(plan, c, cells)
    plane = jacobian_plane(plan, (sq, sa, sb, sc), coef)
    carry = sweep_start(plan, fx)
    stores = []
    for c in range(CHUNKS):
        coefs[c].wait()
        size = plan.z // CHUNKS
        carry = sweep(plan, plane, (out_w, out_h), fx, carry, c * size, size)
        rows = chunk_rows(plan, c)
        stores.append(copies.start(out.at[:, rows], out_back.at[:, rows]))
    if last:
        late.wait()
        groups = (tuple(base.at[i] for i in range(3)), (sq, v1, v2))
        fracs = (base_frac, frac_vec)
        rr, rw = block_sums(plan, groups, fracs, lambda r, w: (r * r, r * w), 2)
        share = safe_ratio(rw, rr)
        (uu,) = block_sums(plan, groups, fracs, lambda r, w: (jnp.square(w - share * r),), 1)
        r11 = jnp.sqrt(rr)
        put_lanes(stats, (r11, safe_ratio(rw, r11), jnp.sqrt(uu), share, uu))
    wait_all(stores)


def put_lanes(out, values):
    lane = lax.broadcasted_iota(jnp.int32, out.shape, 1)
    total = jnp.zeros(out.shape, F32)
    for j, value in enumerate(values):
        total = jnp.where(lane == j, value, total)
    out[...] = total


def jacobian_kernel(plan, last, *refs):
    n, m = len(plan.slots), len(plan.faces)
    refs = list(refs)
    take = lambda count: [refs.pop(0) for _ in range(count)]
    out_in, kb = take(2)
    fp, fs, fd, frac_volume, frac_vec = take(5)
    segment, column, weight, weight_back, own, got, own_vec, recv = take(8)
    own_faces, recv_faces = take(m), take(n)
    own_vec_faces, recv_vec_faces = take(m), take(n)
    if last:
        vec_in, base_in, base_frac, stats_in = take(4)
        (stats,) = take(1)
    else:
        out_back, frac_out = take(2)
        faces = take(m)
        pack, own_out = take(2)
    out, y_store, rates, sems, got_vec = take(5)
    fields = tuple(out.at[i] for i in range(3))
    copies = Copies(sems)
    load = copies.start(out_in, out)
    if last:
        vec, base, frac_out = take(3)
        late = [copies.start(vec_in, vec), copies.start(base_in, base)]

    unpack_pairs(plan, recv, got_vec)

    def pair_rates(weights, seg_values, seg_steps, cell_values, cell_steps):
        w0, h0, _, a0, b0, _ = mobility_steps(*seg_values, *seg_steps)
        w1, h1, _, a1, b1, _ = mobility_steps(*cell_values, *cell_steps)
        drop = seg_values[0] - cell_values[0]
        dq = seg_steps[0] - cell_steps[0]
        half = 0.5 * weights
        return (
            half * ((a0 + a1) * drop + (w0 + w1) * dq),
            half * ((b0 + b1) * drop + (h0 + h1) * dq),
        )

    rate_w, rate_h = pair_rates(
        weight_back[...],
        pair_values(plan, own, 0),
        pair_values(plan, own_vec, 0),
        pair_values(plan, got, 1),
        pair_values(plan, got_vec, 1),
    )
    values = (fp[...], fs[...], fd[...], frac_vec[0], frac_vec[1], frac_vec[2])
    _, _, _, mass_w, mass_h, frac_out[2] = cell_steps(*values)
    vol = frac_volume[...]
    frac_out[0] = vol * mass_w + scatter_segments(plan, rate_w, segment[...])
    frac_out[1] = vol * mass_h + scatter_segments(plan, rate_h, segment[...])
    rate_w, rate_h = pair_rates(
        weight[...],
        pair_values(plan, got, 0),
        pair_values(plan, got_vec, 0),
        pair_values(plan, own, 1),
        pair_values(plan, own_vec, 1),
    )
    rates[0 : plan.z, :] = rate_w
    rates[plan.z : 2 * plan.z, :] = rate_h

    found = merge_faces(plan, own_faces, recv_faces, 3)
    found_vec = merge_faces(plan, own_vec_faces, recv_vec_faces, 3)
    fluxes = []
    for i, ((axis, high, _, mine, theirs), steps) in enumerate(zip(found, found_vec)):
        fluxes.append(
            face_flux(vertical_sign(axis, high), kb[i], mine, theirs, steps[3], steps[4])
        )
    load.wait()
    add_faces(plan, found, fluxes, fields[:2], y_store)
    scatter_cells(plan, rates, column[...], fields[:2], y_store)
    if not last:
        store = copies.start(out, out_back)
        send_parts(plan, fields, frac_out, segment, column, faces, own_out, pack)
        store.wait()
        return
    wait_all(late)
    known = stats_in[0:1, :]
    lane1 = lax.broadcasted_iota(jnp.int32, (1, 128), 1)
    r11, r12, r22, share, uu = (
        jnp.sum(jnp.where(lane1 == j, known, 0.0), axis=1, keepdims=True) for j in range(5)
    )
    three = lambda ref: tuple(ref.at[i] for i in range(3))
    refs3 = (three(base), three(vec), fields)
    fracs3 = (base_frac, frac_vec, frac_out)
    rz, uz = block_sums(
        plan, refs3, fracs3, lambda r, w, v: (r * v, (w - share * r) * v), 2
    )
    along_r, along_u = safe_ratio(rz, r11 * r11), safe_ratio(uz, uu)
    (vv,) = block_sums(
        plan,
        refs3,
        fracs3,
        lambda r, w, v: (jnp.square(v - along_r * r - along_u * (w - share * r)),),
        1,
    )
    put_lanes(stats, (r11, r12, r22, safe_ratio(rz, r11), safe_ratio(uz, r22), jnp.sqrt(vv)))


def step_kernel(plan, stats, res_in, frac_res, vec_in, frac_vec, out, frac_step, *scratch):
    res, vec, step, sems = scratch
    copies = Copies(sems)
    loads = [
        [copies.start(a.at[f], b.at[f]) for a, b in ((res_in, res), (vec_in, vec))]
        for f in range(3)
    ]
    table = stats[...]
    lane = lax.broadcasted_iota(jnp.int32, table.shape, 1)
    r11, r12, r22, r13, r23, r33 = (
        jnp.sum(jnp.where(lane == j, table, 0.0), axis=1, keepdims=True) for j in range(6)
    )
    add = lambda v: jnp.sum(v, axis=0, keepdims=True)
    norm2 = add(r11 * r11) + EPS
    norm = jnp.sqrt(norm2)
    c11 = add(r11 * r12) / norm2
    left1, left2 = r12 - c11 * r11, r22
    c21 = jnp.sqrt(add(left1 * left1 + left2 * left2) / norm2 + EPS)
    scale = 1.0 / (norm * c21)
    second1, second2 = -scale * left1, -scale * left2
    image1 = -scale * (r13 - c11 * r12)
    image2 = -scale * (r23 - c11 * r22)
    image3 = -scale * r33
    first1 = -r11 / norm
    c12 = add(image1 * first1)
    c22 = add(image1 * second1 + image2 * second2)
    u1 = image1 - c12 * first1 - c22 * second1
    u2 = image2 - c22 * second2
    c32_2 = add(u1 * u1 + u2 * u2 + image3 * image3) + EPS
    rho = jnp.sqrt(c11 * c11 + c21 * c21)
    co, si = c11 / rho, c21 / rho
    t1 = co * c12 + si * c22
    t2 = co * c22 - si * c12
    y2 = -si * norm * t2 / (t2 * t2 + c32_2)
    y1 = (co * norm - t1 * y2) / rho
    on_vec = -y2 * scale
    on_res = -y1 / norm - c11 * on_vec
    stores = []
    for f in range(3):
        wait_all(loads[f])

        def body(z, carry):
            here = plane_rows(plan, z)
            step[f, here, :] = on_res * res[f, here, :] + on_vec * vec[f, here, :]
            return carry

        lax.fori_loop(0, plan.z, body, 0, unroll=4)
        stores.append(copies.start(step.at[f], out.at[f]))
    for f in range(3):
        frac_step[f] = on_res * frac_res[f] + on_vec * frac_vec[f]
    wait_all(stores)


def call(kernel, out_shapes, args, scratch, copies, more=(), smem=(), far=(), far_out=(), work=0):
    place = lambda i: pltpu.SMEM if i in smem else pl.ANY if i in far else pltpu.VMEM
    cost = pl.CostEstimate(flops=work, bytes_accessed=work, transcendentals=0) if work else None
    return pl.pallas_call(
        kernel,
        out_shape=[jax.ShapeDtypeStruct(shape, F32) for shape in out_shapes],
        in_specs=[pl.BlockSpec(memory_space=place(i)) for i in range(len(args))],
        out_specs=[
            pl.BlockSpec(memory_space=pl.ANY if i in far_out else pltpu.VMEM)
            for i in range(len(out_shapes))
        ],
        scratch_shapes=[pltpu.VMEM(shape, F32) for shape in scratch]
        + [pltpu.SemaphoreType.DMA((copies,))]
        + [pltpu.VMEM(shape, F32) for shape in more],
        compiler_params=pltpu.CompilerParams(vmem_limit_bytes=56 << 20),
        cost_estimate=cost,
    )(*args)


def on_device(mesh_shape, *args):
    (
        pressure,
        saturation,
        dissolved,
        old_water,
        old_hydrogen,
        pore_volume,
        permeability,
        frac_pressure,
        frac_saturation,
        frac_dissolved,
        frac_old_water,
        frac_old_hydrogen,
        frac_volume,
        pair_segment,
        pair_column,
        pair_kind,
        pair_count,
        transfer_table,
    ) = args
    cap = pair_column.shape[1] // pair_count.shape[1]
    plan = Plan(mesh_shape, pressure, frac_pressure, pair_column, cap)
    slots = len(plan.slots)
    devices = plan.sizes["gx"] * plan.sizes["gy"] * plan.sizes["gz"]
    flat = lambda a: a.reshape(plan.rows, plan.y)
    p, s, d, k = (flat(a) for a in (pressure, saturation, dissolved, permeability))
    volume = flat(pore_volume)
    field = (plan.rows, plan.y)
    padded = (plan.rows + plan.x + 8, plan.y)
    pair_shape = (6 * plan.z, plan.pairs)
    face_count = len(plan.faces)
    sweep_scratch = (2 * UNROLL, plan.x + 8, plan.y)
    y_scratch = (2, plan.x, plan.y)
    rate_scratch = (2 * plan.z, plan.pairs)
    coef_shape = (11,) + field
    three = (3,) + field
    frac_shape = (3, plan.z, plan.seg)
    inner_work = 16 << 20

    def exchange(faces, pack):
        got = lax.all_to_all(pack, PLANE, 0, 0, tiled=True)
        moved = [
            lax.ppermute(faces[spot], axis, swap_pairs(plan.sizes[axis], odd))
            for (axis, odd), spot in zip(plan.slots, plan.slot_face)
        ]
        return moved, got

    outs = call(
        functools.partial(first_kernel, plan),
        [(4, 32, 128)] * face_count
        + [(plan.peers, plan.pack_rows + 8, 128), pair_shape, (1, plan.pairs)],
        [p, s, d, k, frac_pressure, frac_saturation, frac_dissolved]
        + [pair_segment, pair_column, pair_kind, pair_count, transfer_table],
        scratch=[(4,) + field],
        copies=4,
        smem=(10, 11),
        far=(0, 1, 2, 3),
    )
    faces, (pack, own, weight) = outs[:face_count], outs[face_count:]
    recv_faces, recv = exchange(faces, pack)
    res, coef = call(
        functools.partial(residual_inner, plan),
        [three, coef_shape],
        [p, s, d, flat(old_water), flat(old_hydrogen), volume, k, weight],
        scratch=[padded] * 5 + [(5,) + field, three, coef_shape, sweep_scratch],
        copies=9 * CHUNKS,
        far=range(7),
        far_out=(0, 1),
        work=inner_work,
    )
    outs = call(
        functools.partial(residual_kernel, plan),
        [three, frac_shape, (face_count, 32, 128)]
        + [(3, 32, 128)] * face_count
        + [(plan.peers, plan.pack_rows, 128), pair_shape, pair_shape, (1, plan.pairs)],
        [res, frac_pressure, frac_saturation, frac_dissolved]
        + [frac_old_water, frac_old_hydrogen, frac_volume]
        + [pair_segment, pair_column, weight, own, recv]
        + list(faces)
        + list(recv_faces),
        scratch=[three, y_scratch, rate_scratch],
        copies=2,
        far=(0,),
        far_out=(0,),
    )
    res, frac_res, kb = outs[:3]
    vec_faces = outs[3 : 3 + face_count]
    pack, own_vec, got, weight_back = outs[3 + face_count :]

    def image(vec, frac_vec, vec_faces, pack, own_vec, base):
        recv_vec_faces, recv_vec = exchange(vec_faces, pack)
        last = base is not None
        outs = call(
            functools.partial(jacobian_inner, plan, last),
            [three] + ([(8, 128)] if last else []),
            [p, s, d, volume, vec, coef] + ([*base, frac_vec] if last else []),
            scratch=[padded] * 4 + [(6,) + field, coef_shape, three, sweep_scratch],
            more=[three] if last else [],
            copies=9 * CHUNKS + 1,
            far=range(7 if last else 6),
            far_out=(0,),
            work=inner_work,
        )
        args = [outs[0], kb]
        args += [frac_pressure, frac_saturation, frac_dissolved, frac_volume, frac_vec]
        args += [pair_segment, pair_column, weight, weight_back, own, got, own_vec, recv_vec]
        args += list(faces) + list(recv_faces) + list(vec_faces) + list(recv_vec_faces)
        if last:
            far = (0, len(args), len(args) + 1)
            args += [vec, *base, outs[1]]
            shapes = [(devices, 128)]
        else:
            far = (0,)
            shapes = [three, frac_shape] + [(3, 32, 128)] * face_count
            shapes += [(plan.peers, plan.pack_rows, 128), pair_shape]
        return call(
            functools.partial(jacobian_kernel, plan, last),
            shapes,
            args,
            scratch=[three, y_scratch, rate_scratch],
            more=[pair_shape] + ([three, three, frac_shape] if last else []),
            copies=3,
            far=far,
            far_out=() if last else (0,),
        )

    outs = image(res, frac_res, vec_faces, pack, own_vec, None)
    vec, frac_vec = outs[:2]
    vec_faces = outs[2 : 2 + face_count]
    pack, own_vec = outs[2 + face_count :]
    (stats,) = image(vec, frac_vec, vec_faces, pack, own_vec, (res, frac_res))
    stats = lax.all_to_all(stats, ("gx", "gy", "gz"), 0, 0, tiled=True)
    step, frac_step = call(
        functools.partial(step_kernel, plan),
        [three, frac_shape],
        [stats, res, frac_res, vec, frac_vec],
        scratch=[three] * 3,
        copies=9,
        far=(1, 3),
        far_out=(0,),
    )
    shape = (3, plan.z, plan.x, plan.y)
    return step.reshape(shape), frac_step, res.reshape(shape), frac_res


def solution(mesh):
    grid = P("gz", "gx", "gy")
    segments = P("gz", PLANE)
    lists = P(PLANE, None)
    return jax.shard_map(
        functools.partial(on_device, dict(mesh.shape)),
        mesh=mesh,
        in_specs=(grid,) * 7 + (segments,) * 6 + (lists,) * 4 + (P(),),
        out_specs=(
            P(None, "gz", "gx", "gy"),
            P(None, "gz", PLANE),
            P(None, "gz", "gx", "gy"),
            P(None, "gz", PLANE),
        ),
        check_vma=False,
    )
```

```python
import functools

import jax
import jax.numpy as jnp
from jax import lax
from jax.experimental import pallas as pl
from jax.experimental.pallas import tpu as pltpu
from jax.sharding import PartitionSpec as P

F32 = jnp.float32
BF16 = jnp.bfloat16
EPS = 1e-06
PLANE = ("gx", "gy")
VMEM_BYTES = 67043328


def swap_slots(mesh_shape):
    slots = []
    for axis in ("gx", "gy", "gz"):
        if mesh_shape[axis] > 1:
            slots.append((axis, 0))
        if mesh_shape[axis] > 2:
            slots.append((axis, 1))
    return tuple(slots)


def swap_pairs(size, odd):
    pairs = []
    for i in range(size):
        up = i % 2 == odd
        partner = (i + 1 if up else i - 1) % size
        pairs.append((i, partner))
    if sorted(j for _, j in pairs) != list(range(size)):
        pairs = [(i, j if abs(i - j) == 1 else i) for i, j in pairs]
    return pairs


def slot_side(axis, odd, sizes):
    index = lax.axis_index(axis)
    high = lax.rem(index, 2) == odd
    valid = jnp.where(high, index + 1 < sizes[axis], index > 0)
    return high, valid


def mobilities(p, s, d):
    share = (1.0 - s) * (1.0 - s)
    scaled = (1.0 + 0.05 * p) * share
    mg = (2.0 + p) * (s * s)
    return scaled * (1.0 - d), scaled * d + mg, mg


def mobility_steps(p, s, d, dp, ds, dd):
    lb = 1.0 + 0.05 * p
    gas = 2.0 + p
    open_s = 1.0 - s
    scaled = lb * (open_s * open_s)
    mg = gas * (s * s)
    solute = scaled * d
    steps = mobility_moves(lb, gas, open_s, s, d, dp, ds, dd)
    return scaled - solute, solute + mg, mg, steps[0], steps[1], steps[2]


def mobility_moves(lb, gas, open_s, s, d, dp, ds, dd):
    by_s = lb * ds
    move = (0.05 * dp) * open_s - by_s
    move_d = (lb * open_s) * dd
    step = open_s * (move - by_s)
    by_p, by_gas = s * dp, gas * ds
    both = by_p + by_gas
    dmg = s * (both + by_gas)
    dml = step * d + open_s * move_d
    return step - dml, dml + dmg, dmg, move, move_d, 0.1 * both


def cell_steps(p, s, d, dp, ds, dd):
    lb = 1.0 + 0.05 * p
    dmw, dmh, dmg, move, move_d, gas_mass = mobility_moves(
        lb, 2.0 + p, 1.0 - s, s, d, dp, ds, dd
    )
    in_liquid = move * d + move_d
    return dmw, dmh, dmg, move - in_liquid, in_liquid + gas_mass, closure_step(p, s, d, dp, ds, dd)


def masses(p, s, d):
    lb_open = (1.0 + 0.05 * p) * (1.0 - s)
    return lb_open * (1.0 - d), lb_open * d + (0.2 + 0.1 * p) * s


def closure(p, s, d):
    gap = 0.05 + 0.025 * p - d
    return s + gap - jnp.sqrt(s * s + gap * gap + 1e-4)


def closure_step(p, s, d, dp, ds, dd):
    gap = 0.05 + 0.025 * p - d
    inverse = lax.rsqrt(s * s + gap * gap + 1e-4)
    dgap = 0.025 * dp - dd
    return ds + dgap - (s * ds + gap * dgap) * inverse


def halves(value):
    high = value.astype(BF16)
    return high, (value - high.astype(F32)).astype(BF16)


def twice(weights, axis):
    return jnp.concatenate([weights, weights], axis=axis)


def split_dot(value, weights, axis):
    return lax.dot_general(
        jnp.concatenate(halves(value), axis=1),
        weights,
        dimension_numbers=(((1,), (axis,)), ((), ())),
        preferred_element_type=F32,
    )


def one_hot(size, index_row):
    shape = (size, index_row.shape[1])
    rows = lax.broadcasted_iota(jnp.int32, shape, 0)
    return jnp.where(rows == index_row, 1.0, 0.0)


class Plan:
    def __init__(self, mesh_shape, pressure, frac, column, cap):
        self.sizes = dict(mesh_shape)
        self.slots = swap_slots(mesh_shape)
        self.z, self.x, self.y = pressure.shape
        self.seg = frac.shape[1]
        self.pairs = column.shape[1]
        self.peers = self.pairs // cap
        self.cap = cap
        self.rows = self.z * self.x
        self.groups = 128 // cap
        self.pack_rows = 6 * self.z // self.groups
        self.half = self.x // 2
        assert self.y == 128 and self.x == self.z == 32
        assert self.groups == 8 and self.peers % self.groups == 0
        self.faces = []
        for axis, _ in self.slots:
            if axis != "gy" or axis not in self.faces:
                self.faces.append(axis)
        self.slot_face = []
        spot = 0
        for i, (axis, _) in enumerate(self.slots):
            if i and not (axis == "gy" and self.slots[i - 1][0] == "gy"):
                spot += 1
            self.slot_face.append(spot)


def plane_rows(plan, z):
    return pl.ds(pl.multiple_of(z * plan.x, 8), plan.x)


def column_masks(plan, column):
    x, y = lax.div(column, plan.y), lax.rem(column, plan.y)
    wide = one_hot(2 * plan.y, lax.div(x, plan.half) * plan.y + y).astype(BF16)
    return wide, one_hot(plan.half, lax.rem(x, plan.half))


STEP = 8


def gather_cells(plan, fields, column, dst):
    wide, one_x = column_masks(plan, column)
    wide = twice(wide, 0)

    def body(c, carry):
        for f, field in enumerate(fields):
            rows = pl.ds(pl.multiple_of(c * STEP * plan.x, 8), STEP * plan.x)
            value = field[rows, :].reshape(STEP, plan.x, plan.y)
            sides = [
                value[:, i * plan.half : (i + 1) * plan.half].reshape(STEP * plan.half, plan.y)
                for i in (0, 1)
            ]
            got = split_dot(jnp.concatenate(sides, axis=1), wide, 0)
            got = got.reshape(STEP, plan.half, plan.pairs) * one_x[None]
            start = pl.multiple_of((3 + f) * plan.z + c * STEP, 8)
            dst[pl.ds(start, STEP), :] = jnp.sum(got, axis=1)
        return carry

    lax.fori_loop(0, plan.z // STEP, body, 0)


def scatter_cells(plan, rates, column, dsts, y_store):
    wide, one_x = column_masks(plan, column)
    lane = lax.broadcasted_iota(jnp.int32, (plan.x, 128), 1)
    edge = (lane == 0) | (lane == 127)
    wide = twice(wide, 1)

    def body(c, carry):
        for f, dst in enumerate(dsts):
            block = rates[pl.ds(pl.multiple_of(f * plan.z + c * STEP, 8), STEP), :]
            spread = jnp.concatenate(
                [one_x * block[j : j + 1, :] for j in range(STEP)], axis=0
            )
            got = split_dot(spread, wide, 1)
            for j in range(STEP):
                z = c * STEP + j
                here = plane_rows(plan, z)
                rows = slice(j * plan.half, (j + 1) * plan.half)
                off = jnp.concatenate(
                    [got[rows, i * plan.y : (i + 1) * plan.y] for i in (0, 1)], axis=0
                )
                if "gy" in plan.faces:
                    turn = lax.rem(255 - 2 * z, 128)
                    off = off - jnp.where(edge, pltpu.roll(y_store[f], turn, 1), 0.0)
                dst[here, :] = dst[here, :] - off
        return carry

    lax.fori_loop(0, plan.z // STEP, body, 0)


def gather_segments(plan, fields, segment, dst):
    one_s = twice(one_hot(plan.seg, segment).astype(BF16), 0)
    for f, field in enumerate(fields):
        dst[f * plan.z : (f + 1) * plan.z, :] = split_dot(field[...], one_s, 0)


def scatter_segments(plan, rate, segment):
    one_s = twice(one_hot(plan.seg, segment).astype(BF16), 1)
    return split_dot(rate, one_s, 1)


def block_transpose(plan, tiles):
    tiles = list(tiles)
    block = lax.broadcasted_iota(jnp.int32, tiles[0].shape, 1) // plan.cap
    bit = 1
    while bit < plan.groups:
        clear = (block & bit) == 0
        for i in range(plan.groups):
            if i & bit:
                continue
            low, high = tiles[i], tiles[i | bit]
            shift = bit * plan.cap
            tiles[i] = jnp.where(clear, low, pltpu.roll(high, shift, 1))
            tiles[i | bit] = jnp.where(clear, pltpu.roll(low, 128 - shift, 1), high)
        bit *= 2
    return tiles


def pack_pairs(plan, own, dst):
    n = plan.pack_rows
    for half in range(plan.pairs // 128):
        lanes = slice(half * 128, (half + 1) * 128)
        tiles = [own[g * n : (g + 1) * n, lanes] for g in range(plan.groups)]
        for c, tile in enumerate(block_transpose(plan, tiles)):
            dst[half * plan.groups + c, 0:n, :] = tile


def unpack_pairs(plan, src, dst):
    n = plan.pack_rows
    for half in range(plan.pairs // 128):
        lanes = slice(half * 128, (half + 1) * 128)
        tiles = [src[half * plan.groups + c, 0:n, :] for c in range(plan.groups)]
        for g, tile in enumerate(block_transpose(plan, tiles)):
            dst[g * n : (g + 1) * n, lanes] = tile


def write_faces(plan, fields, outs):
    pair = lax.broadcasted_iota(jnp.int32, (plan.x, 128), 1) // 2
    y_out = None
    for (axis, odd), spot in zip(plan.slots, plan.slot_face):
        out = outs[spot]
        high, _ = slot_side(axis, odd, plan.sizes)
        if axis == "gx":
            row = jnp.where(high, plan.x - 1, 0)
            for f, field in enumerate(fields):
                out[f] = field[pl.ds(row, plan.z, stride=plan.x), :]
        elif axis == "gz":
            start = pl.multiple_of(jnp.where(high, (plan.z - 1) * plan.x, 0), 8)
            for f, field in enumerate(fields):
                out[f] = field[pl.ds(start, plan.x), :]
        else:
            y_out = out
    if y_out is None:
        return
    zero = jnp.zeros((plan.x, 128), F32)

    def body(c, carry):
        carry = list(carry)
        for j in range(4):
            z = c * 4 + j
            for f, field in enumerate(fields):
                value = field[plane_rows(plan, z), :]
                carry[f] = jnp.where(pair == z, pltpu.roll(value, 2 * z + 1, 1), carry[f])
        return tuple(carry)

    for f, value in enumerate(lax.fori_loop(0, plan.z // 4, body, (zero,) * len(fields))):
        y_out[f] = value


def merge_faces(plan, own, recv, count):
    lane = lax.broadcasted_iota(jnp.int32, (plan.x, 128), 1)
    even = lane % 2 == 0
    found = []
    y_recv = []
    for i, (axis, odd) in enumerate(plan.slots):
        high, valid = slot_side(axis, odd, plan.sizes)
        mine = tuple(own[plan.slot_face[i]][f] for f in range(count))
        theirs = tuple(recv[i][f] for f in range(count))
        if axis != "gy":
            found.append((axis, high, valid, mine, theirs))
            continue
        y_recv.append((high, theirs))
        if odd or plan.sizes["gy"] == 2:
            first = y_recv[0][0]
            above = tuple(jnp.where(first, a, b) for a, b in zip(y_recv[0][1], y_recv[-1][1]))
            below = tuple(jnp.where(first, b, a) for a, b in zip(y_recv[0][1], y_recv[-1][1]))
            merged = tuple(
                jnp.where(even, pltpu.roll(a, 127, 1), pltpu.roll(b, 1, 1))
                for a, b in zip(above, below)
            )
            index = lax.axis_index("gy")
            up = jnp.where(index + 1 < plan.sizes["gy"], 1, 0)
            down = jnp.where(index > 0, 1, 0)
            inside = jnp.where(even, up, down) * jnp.where(lane < 2 * plan.z, 1, 0)
            found.append((axis, None, inside == 1, mine, merged))
    return found


def vertical_sign(axis, high):
    if axis != "gz":
        return None
    return jnp.where(high, 1.0, -1.0).astype(F32)


def add_faces(plan, faces, fluxes, dsts, y_store):
    for (axis, high, *_), pair in zip(faces, fluxes):
        for i, (dst, flux) in enumerate(zip(dsts, pair)):
            if axis == "gx":
                rows = pl.ds(jnp.where(high, plan.x - 1, 0), plan.z, stride=plan.x)
                dst[rows, :] = dst[rows, :] + flux
            elif axis == "gz":
                start = pl.multiple_of(jnp.where(high, (plan.z - 1) * plan.x, 0), 8)
                rows = pl.ds(start, plan.x)
                dst[rows, :] = dst[rows, :] + flux
            else:
                y_store[i] = flux


UNROLL = 4


def sweep(plan, plane, dsts, fx, carry, first, count):
    def body(c, carry):
        carry = list(carry)
        for u in range(UNROLL):
            z = first + c * UNROLL + u
            here = plane_rows(plan, z)
            for i, (along_y, along_x, along_z) in enumerate(plane(z)):
                slot = 2 * u + i
                total = dsts[i][here, :] + (along_y - pltpu.roll(along_y, 1, 1))
                fx[slot, 8 : 8 + plan.x, :] = along_x
                total = total + (along_x - fx[slot, 7 : 7 + plan.x, :])
                dsts[i][here, :] = total + (along_z - carry[i])
                carry[i] = along_z
        return tuple(carry)

    return lax.fori_loop(0, count // UNROLL, body, carry)


def sweep_start(plan, fx):
    zero = jnp.zeros((plan.x, 128), F32)
    for i in range(2 * UNROLL):
        fx[i, 0:8, :] = jnp.zeros((8, 128), F32)
    return zero, zero


CHUNKS = 4


def chunk_rows(plan, c):
    size = plan.rows // CHUNKS
    return pl.ds(c * size, size)


def chunk_loop(plan, c, body):
    size = plan.z // CHUNKS
    lax.fori_loop(c * size, (c + 1) * size, body, 0)


def residual_plane(plan, base, k_ref, coef):
    p_ref, w_ref, h_ref, g_ref = base
    lane = lax.broadcasted_iota(jnp.int32, (plan.x, 128), 1)
    row = lax.broadcasted_iota(jnp.int32, (plan.x, 128), 0)
    back = lambda v: pltpu.roll(v, 127, 1)

    def plane(z):
        here, below = plane_rows(plan, z), plane_rows(plan, z + 1)
        beside = pl.ds(z * plan.x + 1, plan.x)
        p0, w0, h0, k0 = (r[here, :] for r in (p_ref, w_ref, h_ref, k_ref))
        flows = []
        sides = (
            (0, lane == 127, tuple(back(v) for v in (p0, w0, h0, k0))),
            (3, row == plan.x - 1, tuple(r[beside, :] for r in (p_ref, w_ref, h_ref, k_ref))),
        )
        for spot, last, (p1, w1, h1, k1) in sides:
            k = jnp.where(last, 0.0, k0 * k1 / (k0 + k1))
            drop, w, h = k * (p0 - p1), w0 + w1, h0 + h1
            coef[spot, here, :] = drop
            coef[spot + 1, here, :] = k * w
            coef[spot + 2, here, :] = k * h
            flows.append((drop * w, drop * h))
        p1, w1, h1, k1 = (r[below, :] for r in (p_ref, w_ref, h_ref, k_ref))
        k = jnp.where(z == plan.z - 1, 0.0, 0.2).astype(F32) * (k0 * k1 / (k0 + k1))
        total = 0.0125 * (p0 + p1)
        drop = k * (p0 - p1 + (0.5 + total))
        extra = k * (total - 0.4)
        w, h, g = w0 + w1, h0 + h1, g_ref[here, :] + g_ref[below, :]
        for i, value in enumerate((drop, k * w, k * h, extra, k * g)):
            coef[6 + i, here, :] = value
        flows.append((drop * w, drop * h + extra * g))
        return tuple(zip(*flows))

    return plane


def jacobian_plane(plan, steps, coef):
    q_ref, a_ref, b_ref, c_ref = steps
    back = lambda v: pltpu.roll(v, 127, 1)

    def plane(z):
        here, below = plane_rows(plan, z), plane_rows(plan, z + 1)
        beside = pl.ds(z * plan.x + 1, plan.x)
        q0, a0, b0 = q_ref[here, :], a_ref[here, :], b_ref[here, :]
        flows = []
        sides = (
            (0, tuple(back(v) for v in (q0, a0, b0))),
            (3, tuple(r[beside, :] for r in (q_ref, a_ref, b_ref))),
        )
        for spot, (q1, a1, b1) in sides:
            drop, w, h = (coef[spot + i, here, :] for i in range(3))
            dq = q0 - q1
            flows.append(((a0 + a1) * drop + w * dq, (b0 + b1) * drop + h * dq))
        q1, a1, b1 = q_ref[below, :], a_ref[below, :], b_ref[below, :]
        drop, w, h, extra, g = (coef[6 + i, here, :] for i in range(5))
        dtotal = 0.0125 * (q0 + q1)
        dq = q0 - q1 + dtotal
        c = c_ref[here, :] + c_ref[below, :]
        flows.append(
            ((a0 + a1) * drop + w * dq, (b0 + b1) * drop + h * dq + (c * extra + g * dtotal))
        )
        return tuple(zip(*flows))

    return plane


class Copies:
    def __init__(self, sems):
        self.sems, self.used = sems, 0

    def start(self, src, dst):
        copy = pltpu.make_async_copy(src, dst, self.sems.at[self.used])
        self.used += 1
        copy.start()
        return copy


def wait_all(copies):
    for copy in copies:
        copy.wait()


class Transfers:
    def __init__(self, sems):
        self.copies = Copies(sems)
        self.loads, self.results, self.stores = {}, {}, []

    def load(self, src, dst):
        self.loads[id(dst)] = self.copies.start(src, dst)

    def result(self, src, dst):
        self.results[id(src)] = (src, dst)

    def ready(self, *refs):
        for ref in refs:
            copy = self.loads.pop(id(ref), None)
            if copy is not None:
                copy.wait()

    def done(self, *refs):
        for ref in refs:
            self.stores.append(self.copies.start(*self.results.pop(id(ref))))

    def finish(self):
        wait_all(list(self.loads.values()))
        for src, dst in self.results.values():
            self.stores.append(self.copies.start(src, dst))
        wait_all(self.stores)


def clear_tails(plan, refs):
    for ref in refs:
        ref[plan.rows : plan.rows + plan.x + 8, :] = jnp.zeros((plan.x + 8, 128), F32)


def face_flux(sign, conductance, own, other, own_step=None, other_step=None):
    p0, p1 = own[0], other[0]
    if own_step is None:
        (w0, h0, g0), (w1, h1, g1) = mobilities(*own), mobilities(*other)
    else:
        w0, h0, g0, a0, b0, c0 = mobility_steps(*own, *own_step)
        w1, h1, g1, a1, b1, c1 = mobility_steps(*other, *other_step)
        q0, q1 = own_step[0], other_step[0]
    drop = p0 - p1
    if sign is not None:
        total = 0.0125 * (p0 + p1)
        drop = drop + sign * (0.5 + total)
        extra = sign * (total - 0.4)
    if own_step is None:
        water = (w0 + w1) * drop
        hydrogen = (h0 + h1) * drop
        if sign is not None:
            hydrogen = hydrogen + (g0 + g1) * extra
        return conductance * water, conductance * hydrogen
    dq = q0 - q1
    if sign is not None:
        dtotal = sign * (0.0125 * (q0 + q1))
        dq = dq + dtotal
    water = (a0 + a1) * drop + (w0 + w1) * dq
    hydrogen = (b0 + b1) * drop + (h0 + h1) * dq
    if sign is not None:
        hydrogen = hydrogen + (c0 + c1) * extra + (g0 + g1) * dtotal
    return conductance * water, conductance * hydrogen


def first_kernel(plan, io, *refs):
    n = len(plan.faces)
    grids = refs[:4]
    fp, fs, fd, segment, column, kind, count, table = refs[4:12]
    faces, (pack, own, weight) = refs[12 : 12 + n], refs[12 + n : 15 + n]
    local, sems = refs[15 + n :]
    copies = Copies(sems)
    loads = [copies.start(g, local.at[i]) for i, g in enumerate(grids)]
    io.ready(fp, fs, fd, segment, kind, column)
    gather_segments(plan, (fp, fs, fd), segment[...], own)
    kinds = kind[...]
    picked = jnp.zeros(kinds.shape, F32)
    for j in range(table.shape[0]):
        picked = jnp.where(kinds == j, table[j], picked)
    slot = lax.broadcasted_iota(jnp.int32, kinds.shape, 1)
    block, rank = slot // plan.cap, lax.rem(slot, plan.cap)
    live = jnp.zeros(kinds.shape, jnp.int32)
    for j in range(plan.peers):
        live = jnp.where(block == j, count[0, j], live)
    picked = jnp.where(rank < live, picked, 0.0)
    weight[...] = picked
    for half in range(plan.pairs // 128):
        tile = jnp.broadcast_to(picked[:, half * 128 : (half + 1) * 128], (8, 128))
        for c in range(plan.groups):
            moved = pltpu.roll(tile, 128 - c * plan.cap, 1) if c else tile
            pack[half * plan.groups + c, plan.pack_rows : plan.pack_rows + 8, :] = moved
    wait_all(loads[:3])
    fields = tuple(local.at[i] for i in range(4))
    gather_cells(plan, fields[:3], column[...], own)
    pack_pairs(plan, own, pack)
    io.done(own, pack, weight)
    wait_all(loads[3:])
    write_faces(plan, fields, faces)


def pair_values(plan, ref, side):
    first = 3 * side
    return tuple(ref[(first + f) * plan.z : (first + f + 1) * plan.z, :] for f in range(3))


def residual_inner(plan, io, *refs):
    grids, (_, res_out, coef_out) = refs[:7], refs[7:10]
    sp, sk, sw, sh, sg, local, res, coef, fx, sems = refs[10:]
    copies = Copies(sems)
    places = [sp] + [local.at[i] for i in range(5)] + [sk]
    loads = [
        [
            copies.start(grid.at[chunk_rows(plan, c)], place.at[chunk_rows(plan, c)])
            for grid, place in zip(grids, places)
        ]
        for c in range(CHUNKS)
    ]
    s, d, old_water, old_hydrogen, volume = (local.at[i] for i in range(5))
    res_w, res_h, res_c = (res.at[i] for i in range(3))
    clear_tails(plan, (sp, sw, sh, sg))
    sk[plan.rows : plan.rows + plan.x + 8, :] = jnp.ones((plan.x + 8, 128), F32)

    def cells(z, carry):
        here = plane_rows(plan, z)
        pv, sv, dv = sp[here, :], s[here, :], d[here, :]
        sw[here, :], sh[here, :], sg[here, :] = mobilities(pv, sv, dv)
        mw, mh = masses(pv, sv, dv)
        vol = volume[here, :]
        res_w[here, :] = vol * (mw - old_water[here, :])
        res_h[here, :] = vol * (mh - old_hydrogen[here, :])
        res_c[here, :] = closure(pv, sv, dv)
        return carry

    for c in range(CHUNKS):
        wait_all(loads[c])
        chunk_loop(plan, c, cells)
    plane = residual_plane(plan, (sp, sw, sh, sg), sk, coef)
    carry = sweep_start(plan, fx)
    stores = []
    for c in range(CHUNKS):
        size = plan.z // CHUNKS
        carry = sweep(plan, plane, (res_w, res_h), fx, carry, c * size, size)
        rows = chunk_rows(plan, c)
        stores.append(copies.start(res.at[:, rows], res_out.at[:, rows]))
        stores.append(copies.start(coef.at[:, rows], coef_out.at[:, rows]))
    wait_all(stores)


def residual_kernel(plan, io, *refs):
    n, m = len(plan.slots), len(plan.faces)
    refs = list(refs)
    take = lambda count: [refs.pop(0) for _ in range(count)]
    (res_in,) = take(1)
    fp, fs, fd, frac_water, frac_hydrogen, frac_volume = take(6)
    segment, column, weight, own, recv = take(5)
    own_faces, recv_faces = take(m), take(n)
    res_out, frac_res, kb = take(3)
    faces = take(m)
    pack, own_res, got, weight_back = take(4)
    res, y_store, rates, sems = take(4)
    fields = tuple(res.at[i] for i in range(3))
    copies = Copies(sems)
    load = copies.start(res_in, res)

    io.ready(recv)
    unpack_pairs(plan, recv, got)
    lane8 = lax.broadcasted_iota(jnp.int32, (8, 128), 1) // plan.cap
    for half in range(plan.pairs // 128):
        total = None
        for c in range(plan.groups):
            tile = recv[half * plan.groups + c, plan.pack_rows : plan.pack_rows + 8, :]
            moved = pltpu.roll(tile, c * plan.cap, 1) if c else tile
            total = moved if total is None else jnp.where(lane8 == c, moved, total)
        weight_back[:, half * 128 : (half + 1) * 128] = total[0:1, :]
    io.done(got, weight_back)
    io.ready(own, weight, segment, column, fp, fs, fd)
    io.ready(frac_water, frac_hydrogen, frac_volume)

    def pair_rates(weights, seg_values, cell_values):
        w0, h0, _ = mobilities(*seg_values)
        w1, h1, _ = mobilities(*cell_values)
        flow = (0.5 * weights) * (seg_values[0] - cell_values[0])
        return flow * (w0 + w1), flow * (h0 + h1)

    rate_w, rate_h = pair_rates(
        weight_back[...], pair_values(plan, own, 0), pair_values(plan, got, 1)
    )
    fpv, fsv, fdv = fp[...], fs[...], fd[...]
    mass_w, mass_h = masses(fpv, fsv, fdv)
    vol = frac_volume[...]
    frac_res[0] = vol * (mass_w - frac_water[...]) + scatter_segments(plan, rate_w, segment[...])
    frac_res[1] = vol * (mass_h - frac_hydrogen[...]) + scatter_segments(
        plan, rate_h, segment[...]
    )
    frac_res[2] = closure(fpv, fsv, fdv)
    io.done(frac_res)
    rate_w, rate_h = pair_rates(weight[...], pair_values(plan, got, 0), pair_values(plan, own, 1))
    rates[0 : plan.z, :] = rate_w
    rates[plan.z : 2 * plan.z, :] = rate_h

    io.ready(*own_faces, *recv_faces)
    found = merge_faces(plan, own_faces, recv_faces, 4)
    fluxes = []
    for i, (axis, high, valid, mine, theirs) in enumerate(found):
        k0, k1 = mine[3], theirs[3]
        scale = 0.2 if axis == "gz" else 1.0
        conductance = jnp.where(
            valid, scale * (k0 * k1 / jnp.where(valid, k0 + k1, 1.0)), 0.0
        )
        kb[i] = conductance
        fluxes.append(face_flux(vertical_sign(axis, high), conductance, mine[:3], theirs[:3]))
    io.done(kb)
    load.wait()
    add_faces(plan, found, fluxes, fields[:2], y_store)
    scatter_cells(plan, rates, column[...], fields[:2], y_store)
    store = copies.start(res, res_out)
    send_parts(plan, io, fields, frac_res, segment, column, faces, own_res, pack)
    store.wait()


def send_parts(plan, io, fields, frac_fields, segment, column, faces, own, pack):
    gather_segments(plan, tuple(frac_fields.at[i] for i in range(3)), segment[...], own)
    gather_cells(plan, fields, column[...], own)
    pack_pairs(plan, own, pack)
    io.done(own, pack)
    write_faces(plan, fields, faces)
    io.done(*faces)


def total_of(value):
    return jnp.sum(jnp.sum(value, axis=0, keepdims=True), axis=1, keepdims=True)


def block_sums(plan, cell_refs, frac_refs, function, count):
    def body(z, carry):
        here = plane_rows(plan, z)
        for f in range(3):
            parts = function(*(group[f][here, :] for group in cell_refs))
            carry = tuple(c + part for c, part in zip(carry, parts))
        return carry

    zero = jnp.zeros((plan.x, 128), F32)
    sums = lax.fori_loop(0, plan.z, body, (zero,) * count, unroll=2)
    sums = [total_of(v) for v in sums]
    for f in range(3):
        parts = function(*(ref[f] for ref in frac_refs))
        sums = [v + total_of(part) for v, part in zip(sums, parts)]
    return sums


def safe_ratio(top, bottom):
    good = bottom > 0.0
    return jnp.where(good, top / jnp.where(good, bottom, 1.0), 0.0)


def jacobian_inner(plan, last, io, *refs):
    refs = list(refs)
    take = lambda count: [refs.pop(0) for _ in range(count)]
    grids = take(4)
    vec_in, coef_in = take(2)
    if last:
        base_in, base_frac, frac_vec = take(3)
        out_back, stats = take(2)
    else:
        (out_back,) = take(1)
    sq, sa, sb, sc, local, coef, out, fx, sems = take(9)
    copies = Copies(sems)
    places = [sq] + [local.at[i] for i in range(6)]
    sources = [vec_in.at[i] for i in range(3)] + list(grids)
    loads = [
        [
            copies.start(grid.at[chunk_rows(plan, c)], place.at[chunk_rows(plan, c)])
            for grid, place in zip(sources, places)
        ]
        for c in range(CHUNKS)
    ]
    coefs = [
        copies.start(coef_in.at[:, chunk_rows(plan, c)], coef.at[:, chunk_rows(plan, c)])
        for c in range(CHUNKS)
    ]
    if last:
        (base,) = take(1)
        late = copies.start(base_in, base)
    v1, v2, p, s, d, volume = (local.at[i] for i in range(6))
    out_w, out_h, out_c = (out.at[i] for i in range(3))
    clear_tails(plan, (sq, sa, sb, sc))

    def cells(z, carry):
        here = plane_rows(plan, z)
        values = tuple(r[here, :] for r in (p, s, d, sq, v1, v2))
        sa[here, :], sb[here, :], sc[here, :], mw, mh, out_c[here, :] = cell_steps(*values)
        vol = volume[here, :]
        out_w[here, :] = vol * mw
        out_h[here, :] = vol * mh
        return carry

    for c in range(CHUNKS):
        wait_all(loads[c])
        chunk_loop(plan, c, cells)
    plane = jacobian_plane(plan, (sq, sa, sb, sc), coef)
    carry = sweep_start(plan, fx)
    stores = []
    for c in range(CHUNKS):
        coefs[c].wait()
        size = plan.z // CHUNKS
        carry = sweep(plan, plane, (out_w, out_h), fx, carry, c * size, size)
        rows = chunk_rows(plan, c)
        stores.append(copies.start(out.at[:, rows], out_back.at[:, rows]))
    if last:
        late.wait()
        io.ready(base_frac, frac_vec)
        groups = (tuple(base.at[i] for i in range(3)), (sq, v1, v2))
        fracs = (base_frac, frac_vec)
        rr, rw = block_sums(plan, groups, fracs, lambda r, w: (r * r, r * w), 2)
        share = safe_ratio(rw, rr)
        (uu,) = block_sums(plan, groups, fracs, lambda r, w: (jnp.square(w - share * r),), 1)
        r11 = jnp.sqrt(rr)
        put_lanes(stats, (r11, safe_ratio(rw, r11), jnp.sqrt(uu), share, uu))
    wait_all(stores)


def put_lanes(out, values):
    lane = lax.broadcasted_iota(jnp.int32, out.shape, 1)
    total = jnp.zeros(out.shape, F32)
    for j, value in enumerate(values):
        total = jnp.where(lane == j, value, total)
    out[...] = total


def jacobian_kernel(plan, last, io, *refs):
    n, m = len(plan.slots), len(plan.faces)
    refs = list(refs)
    take = lambda count: [refs.pop(0) for _ in range(count)]
    out_in, kb = take(2)
    fp, fs, fd, frac_volume, frac_vec = take(5)
    segment, column, weight, weight_back, own, got, own_vec, recv = take(8)
    own_faces, recv_faces = take(m), take(n)
    own_vec_faces, recv_vec_faces = take(m), take(n)
    if last:
        vec_in, base_in, base_frac, stats_in = take(4)
        (stats,) = take(1)
    else:
        out_back, frac_out = take(2)
        faces = take(m)
        pack, own_out = take(2)
    out, y_store, rates, sems, got_vec = take(5)
    fields = tuple(out.at[i] for i in range(3))
    copies = Copies(sems)
    load = copies.start(out_in, out)
    if last:
        vec, base, frac_out = take(3)
        late = [copies.start(vec_in, vec), copies.start(base_in, base)]

    io.ready(recv)
    unpack_pairs(plan, recv, got_vec)
    io.ready(own, got, own_vec, weight, weight_back, segment, column)
    io.ready(fp, fs, fd, frac_volume, frac_vec)

    def pair_rates(weights, seg_values, seg_steps, cell_values, cell_steps):
        w0, h0, _, a0, b0, _ = mobility_steps(*seg_values, *seg_steps)
        w1, h1, _, a1, b1, _ = mobility_steps(*cell_values, *cell_steps)
        drop = seg_values[0] - cell_values[0]
        dq = seg_steps[0] - cell_steps[0]
        half = 0.5 * weights
        return (
            half * ((a0 + a1) * drop + (w0 + w1) * dq),
            half * ((b0 + b1) * drop + (h0 + h1) * dq),
        )

    rate_w, rate_h = pair_rates(
        weight_back[...],
        pair_values(plan, own, 0),
        pair_values(plan, own_vec, 0),
        pair_values(plan, got, 1),
        pair_values(plan, got_vec, 1),
    )
    values = (fp[...], fs[...], fd[...], frac_vec[0], frac_vec[1], frac_vec[2])
    _, _, _, mass_w, mass_h, frac_out[2] = cell_steps(*values)
    vol = frac_volume[...]
    frac_out[0] = vol * mass_w + scatter_segments(plan, rate_w, segment[...])
    frac_out[1] = vol * mass_h + scatter_segments(plan, rate_h, segment[...])
    if not last:
        io.done(frac_out)
    rate_w, rate_h = pair_rates(
        weight[...],
        pair_values(plan, got, 0),
        pair_values(plan, got_vec, 0),
        pair_values(plan, own, 1),
        pair_values(plan, own_vec, 1),
    )
    rates[0 : plan.z, :] = rate_w
    rates[plan.z : 2 * plan.z, :] = rate_h

    io.ready(*own_faces, *recv_faces, *own_vec_faces, *recv_vec_faces, kb)
    found = merge_faces(plan, own_faces, recv_faces, 3)
    found_vec = merge_faces(plan, own_vec_faces, recv_vec_faces, 3)
    fluxes = []
    for i, ((axis, high, _, mine, theirs), steps) in enumerate(zip(found, found_vec)):
        fluxes.append(
            face_flux(vertical_sign(axis, high), kb[i], mine, theirs, steps[3], steps[4])
        )
    load.wait()
    add_faces(plan, found, fluxes, fields[:2], y_store)
    scatter_cells(plan, rates, column[...], fields[:2], y_store)
    if not last:
        store = copies.start(out, out_back)
        send_parts(plan, io, fields, frac_out, segment, column, faces, own_out, pack)
        store.wait()
        return
    wait_all(late)
    io.ready(base_frac, stats_in)
    known = stats_in[0:1, :]
    lane1 = lax.broadcasted_iota(jnp.int32, (1, 128), 1)
    r11, r12, r22, share, uu = (
        jnp.sum(jnp.where(lane1 == j, known, 0.0), axis=1, keepdims=True) for j in range(5)
    )
    three = lambda ref: tuple(ref.at[i] for i in range(3))
    refs3 = (three(base), three(vec), fields)
    fracs3 = (base_frac, frac_vec, frac_out)
    rz, uz = block_sums(
        plan, refs3, fracs3, lambda r, w, v: (r * v, (w - share * r) * v), 2
    )
    along_r, along_u = safe_ratio(rz, r11 * r11), safe_ratio(uz, uu)
    (vv,) = block_sums(
        plan,
        refs3,
        fracs3,
        lambda r, w, v: (jnp.square(v - along_r * r - along_u * (w - share * r)),),
        1,
    )
    put_lanes(stats, (r11, r12, r22, safe_ratio(rz, r11), safe_ratio(uz, r22), jnp.sqrt(vv)))


def step_kernel(plan, io, stats, res_in, frac_res, vec_in, frac_vec, out, frac_step, *scratch):
    res, vec, step, sems = scratch
    copies = Copies(sems)
    loads = [
        [copies.start(a.at[f], b.at[f]) for a, b in ((res_in, res), (vec_in, vec))]
        for f in range(3)
    ]
    io.ready(stats)
    table = stats[...]
    lane = lax.broadcasted_iota(jnp.int32, table.shape, 1)
    r11, r12, r22, r13, r23, r33 = (
        jnp.sum(jnp.where(lane == j, table, 0.0), axis=1, keepdims=True) for j in range(6)
    )
    add = lambda v: jnp.sum(v, axis=0, keepdims=True)
    norm2 = add(r11 * r11) + EPS
    norm = jnp.sqrt(norm2)
    c11 = add(r11 * r12) / norm2
    left1, left2 = r12 - c11 * r11, r22
    c21 = jnp.sqrt(add(left1 * left1 + left2 * left2) / norm2 + EPS)
    scale = 1.0 / (norm * c21)
    second1, second2 = -scale * left1, -scale * left2
    image1 = -scale * (r13 - c11 * r12)
    image2 = -scale * (r23 - c11 * r22)
    image3 = -scale * r33
    first1 = -r11 / norm
    c12 = add(image1 * first1)
    c22 = add(image1 * second1 + image2 * second2)
    u1 = image1 - c12 * first1 - c22 * second1
    u2 = image2 - c22 * second2
    c32_2 = add(u1 * u1 + u2 * u2 + image3 * image3) + EPS
    rho = jnp.sqrt(c11 * c11 + c21 * c21)
    co, si = c11 / rho, c21 / rho
    t1 = co * c12 + si * c22
    t2 = co * c22 - si * c12
    y2 = -si * norm * t2 / (t2 * t2 + c32_2)
    y1 = (co * norm - t1 * y2) / rho
    on_vec = -y2 * scale
    on_res = -y1 / norm - c11 * on_vec
    stores = []
    for f in range(3):
        wait_all(loads[f])

        def body(z, carry):
            here = plane_rows(plan, z)
            step[f, here, :] = on_res * res[f, here, :] + on_vec * vec[f, here, :]
            return carry

        lax.fori_loop(0, plan.z, body, 0, unroll=4)
        stores.append(copies.start(step.at[f], out.at[f]))
    io.ready(frac_res, frac_vec)
    for f in range(3):
        frac_step[f] = on_res * frac_res[f] + on_vec * frac_vec[f]
    wait_all(stores)


def call(
    kernel,
    out_shapes,
    args,
    scratch,
    copies,
    more=(),
    smem=(),
    far=(),
    far_out=(),
    first=(),
    work=0,
):
    place = lambda i: pltpu.SMEM if i in smem else pl.ANY
    cost = pl.CostEstimate(flops=work, bytes_accessed=work, transcendentals=0) if work else None
    near = [i for i in first + tuple(range(len(args))) if i not in smem and i not in far]
    near = list(dict.fromkeys(near))
    near_out = [i for i in range(len(out_shapes)) if i not in far_out]

    def body(*refs):
        refs = list(refs)
        take = lambda count: [refs.pop(0) for _ in range(count)]
        ins, outs = take(len(args)), take(len(out_shapes))
        own = take(len(scratch) + 1 + len(more))
        io = Transfers(refs[-1])
        for i in near:
            buffer = refs.pop(0)
            io.load(ins[i], buffer)
            ins[i] = buffer
        for i in near_out:
            buffer = refs.pop(0)
            io.result(buffer, outs[i])
            outs[i] = buffer
        kernel(io, *ins, *outs, *own)
        io.finish()

    return pl.pallas_call(
        body,
        out_shape=[jax.ShapeDtypeStruct(shape, F32) for shape in out_shapes],
        in_specs=[pl.BlockSpec(memory_space=place(i)) for i in range(len(args))],
        out_specs=[pl.BlockSpec(memory_space=pl.ANY)] * len(out_shapes),
        scratch_shapes=[pltpu.VMEM(shape, F32) for shape in scratch]
        + [pltpu.SemaphoreType.DMA((copies,))]
        + [pltpu.VMEM(shape, F32) for shape in more]
        + [pltpu.VMEM(args[i].shape, args[i].dtype) for i in near]
        + [pltpu.VMEM(out_shapes[i], F32) for i in near_out]
        + [pltpu.SemaphoreType.DMA((len(near) + len(near_out) + 1,))],
        compiler_params=pltpu.CompilerParams(vmem_limit_bytes=VMEM_BYTES),
        cost_estimate=cost,
    )(*args)


def on_device(mesh_shape, *args):
    (
        pressure,
        saturation,
        dissolved,
        old_water,
        old_hydrogen,
        pore_volume,
        permeability,
        frac_pressure,
        frac_saturation,
        frac_dissolved,
        frac_old_water,
        frac_old_hydrogen,
        frac_volume,
        pair_segment,
        pair_column,
        pair_kind,
        pair_count,
        transfer_table,
    ) = args
    cap = pair_column.shape[1] // pair_count.shape[1]
    plan = Plan(mesh_shape, pressure, frac_pressure, pair_column, cap)
    slots = len(plan.slots)
    devices = plan.sizes["gx"] * plan.sizes["gy"] * plan.sizes["gz"]
    flat = lambda a: a.reshape(plan.rows, plan.y)
    p, s, d, k = (flat(a) for a in (pressure, saturation, dissolved, permeability))
    volume = flat(pore_volume)
    field = (plan.rows, plan.y)
    padded = (plan.rows + plan.x + 8, plan.y)
    pair_shape = (6 * plan.z, plan.pairs)
    face_count = len(plan.faces)
    sweep_scratch = (2 * UNROLL, plan.x + 8, plan.y)
    y_scratch = (2, plan.x, plan.y)
    rate_scratch = (2 * plan.z, plan.pairs)
    coef_shape = (11,) + field
    three = (3,) + field
    frac_shape = (3, plan.z, plan.seg)
    inner_work = 16 << 20

    def exchange(faces, pack):
        got = lax.all_to_all(pack, PLANE, 0, 0, tiled=True)
        moved = [
            lax.ppermute(faces[spot], axis, swap_pairs(plan.sizes[axis], odd))
            for (axis, odd), spot in zip(plan.slots, plan.slot_face)
        ]
        return moved, got

    outs = call(
        functools.partial(first_kernel, plan),
        [(4, 32, 128)] * face_count
        + [(plan.peers, plan.pack_rows + 8, 128), pair_shape, (1, plan.pairs)],
        [p, s, d, k, frac_pressure, frac_saturation, frac_dissolved]
        + [pair_segment, pair_column, pair_kind, pair_count, transfer_table],
        scratch=[(4,) + field],
        copies=4,
        smem=(10, 11),
        far=(0, 1, 2, 3),
    )
    faces, (pack, own, weight) = outs[:face_count], outs[face_count:]
    recv_faces, recv = exchange(faces, pack)
    res, coef = call(
        functools.partial(residual_inner, plan),
        [three, coef_shape],
        [p, s, d, flat(old_water), flat(old_hydrogen), volume, k, weight],
        scratch=[padded] * 5 + [(5,) + field, three, coef_shape, sweep_scratch],
        copies=9 * CHUNKS,
        far=range(7),
        far_out=(0, 1),
        work=inner_work,
    )
    outs = call(
        functools.partial(residual_kernel, plan),
        [three, frac_shape, (face_count, 32, 128)]
        + [(3, 32, 128)] * face_count
        + [(plan.peers, plan.pack_rows, 128), pair_shape, pair_shape, (1, plan.pairs)],
        [res, frac_pressure, frac_saturation, frac_dissolved]
        + [frac_old_water, frac_old_hydrogen, frac_volume]
        + [pair_segment, pair_column, weight, own, recv]
        + list(faces)
        + list(recv_faces),
        scratch=[three, y_scratch, rate_scratch],
        copies=2,
        far=(0,),
        far_out=(0,),
        first=(11, 10, 9),
    )
    res, frac_res, kb = outs[:3]
    vec_faces = outs[3 : 3 + face_count]
    pack, own_vec, got, weight_back = outs[3 + face_count :]

    def image(vec, frac_vec, vec_faces, pack, own_vec, base):
        recv_vec_faces, recv_vec = exchange(vec_faces, pack)
        last = base is not None
        outs = call(
            functools.partial(jacobian_inner, plan, last),
            [three] + ([(8, 128)] if last else []),
            [p, s, d, volume, vec, coef] + ([*base, frac_vec] if last else []),
            scratch=[padded] * 4 + [(6,) + field, coef_shape, three, sweep_scratch],
            more=[three] if last else [],
            copies=9 * CHUNKS + 1,
            far=range(7 if last else 6),
            far_out=(0,),
            work=inner_work,
        )
        args = [outs[0], kb]
        args += [frac_pressure, frac_saturation, frac_dissolved, frac_volume, frac_vec]
        args += [pair_segment, pair_column, weight, weight_back, own, got, own_vec, recv_vec]
        args += list(faces) + list(recv_faces) + list(vec_faces) + list(recv_vec_faces)
        if last:
            far = (0, len(args), len(args) + 1)
            args += [vec, *base, outs[1]]
            shapes = [(devices, 128)]
        else:
            far = (0,)
            shapes = [three, frac_shape] + [(3, 32, 128)] * face_count
            shapes += [(plan.peers, plan.pack_rows, 128), pair_shape]
        return call(
            functools.partial(jacobian_kernel, plan, last),
            shapes,
            args,
            scratch=[three, y_scratch, rate_scratch],
            more=[pair_shape] + ([three, three, frac_shape] if last else []),
            copies=3,
            far=far,
            far_out=() if last else (0,),
            first=(14, 11, 12, 13),
        )

    outs = image(res, frac_res, vec_faces, pack, own_vec, None)
    vec, frac_vec = outs[:2]
    vec_faces = outs[2 : 2 + face_count]
    pack, own_vec = outs[2 + face_count :]
    (stats,) = image(vec, frac_vec, vec_faces, pack, own_vec, (res, frac_res))
    stats = lax.all_to_all(stats, ("gx", "gy", "gz"), 0, 0, tiled=True)
    step, frac_step = call(
        functools.partial(step_kernel, plan),
        [three, frac_shape],
        [stats, res, frac_res, vec, frac_vec],
        scratch=[three] * 3,
        copies=9,
        far=(1, 3),
        far_out=(0,),
    )
    shape = (3, plan.z, plan.x, plan.y)
    return step.reshape(shape), frac_step, res.reshape(shape), frac_res


def solution(mesh):
    grid = P("gz", "gx", "gy")
    segments = P("gz", PLANE)
    lists = P(PLANE, None)
    return jax.shard_map(
        functools.partial(on_device, dict(mesh.shape)),
        mesh=mesh,
        in_specs=(grid,) * 7 + (segments,) * 6 + (lists,) * 4 + (P(),),
        out_specs=(
            P(None, "gz", "gx", "gy"),
            P(None, "gz", PLANE),
            P(None, "gz", "gx", "gy"),
            P(None, "gz", PLANE),
        ),
        check_vma=False,
    )
```

```python
import functools

import jax
import jax.numpy as jnp
from jax import lax
from jax.experimental import pallas as pl
from jax.experimental.pallas import tpu as pltpu
from jax.sharding import PartitionSpec as P

F32 = jnp.float32
BF16 = jnp.bfloat16
EPS = 1e-06
PLANE = ("gx", "gy")
DEVICES = ("gx", "gy", "gz")
VMEM_BYTES = 67043328


def swap_slots(mesh_shape):
    slots = []
    for axis in ("gx", "gy", "gz"):
        if mesh_shape[axis] > 1:
            slots.append((axis, 0))
        if mesh_shape[axis] > 2:
            slots.append((axis, 1))
    return tuple(slots)


def swap_pairs(sizes, axis, odd):
    pairs = []
    for x in range(sizes["gx"]):
        for y in range(sizes["gy"]):
            for z in range(sizes["gz"]):
                spot = {"gx": x, "gy": y, "gz": z}
                index = spot[axis] + (1 if spot[axis] % 2 == odd else -1)
                other = dict(spot, **{axis: index})
                if not 0 <= index < sizes[axis]:
                    other = dict(spot, gz=(z + 1 if z % 2 == 0 else z - 1))
                    if other["gz"] >= sizes["gz"] or axis == "gz":
                        other = spot
                rank = lambda at: (at["gx"] * sizes["gy"] + at["gy"]) * sizes["gz"] + at["gz"]
                pairs.append((rank(spot), rank(other)))
    return pairs


def slot_side(axis, odd, sizes):
    index = lax.axis_index(axis)
    high = lax.rem(index, 2) == odd
    valid = jnp.where(high, index + 1 < sizes[axis], index > 0)
    return high, valid


def mobilities(p, s, d):
    share = (1.0 - s) * (1.0 - s)
    scaled = (1.0 + 0.05 * p) * share
    mg = (2.0 + p) * (s * s)
    return scaled * (1.0 - d), scaled * d + mg, mg


def mobility_moves(lb, gas, open_s, s, d, dp, ds, dd):
    by_s = lb * ds
    move = (0.05 * dp) * open_s - by_s
    move_d = (lb * open_s) * dd
    step = open_s * (move - by_s)
    by_p, by_gas = s * dp, gas * ds
    both = by_p + by_gas
    dmg = s * (both + by_gas)
    dml = step * d + open_s * move_d
    return step - dml, dml + dmg, dmg, move, move_d, 0.1 * both


def cell_steps(p, s, d, dp, ds, dd):
    lb = 1.0 + 0.05 * p
    dmw, dmh, dmg, move, move_d, gas_mass = mobility_moves(
        lb, 2.0 + p, 1.0 - s, s, d, dp, ds, dd
    )
    in_liquid = move * d + move_d
    return dmw, dmh, dmg, move - in_liquid, in_liquid + gas_mass, closure_step(p, s, d, dp, ds, dd)


def masses(p, s, d):
    lb_open = (1.0 + 0.05 * p) * (1.0 - s)
    return lb_open * (1.0 - d), lb_open * d + (0.2 + 0.1 * p) * s


def closure(p, s, d):
    gap = 0.05 + 0.025 * p - d
    return s + gap - jnp.sqrt(s * s + gap * gap + 1e-4)


def closure_step(p, s, d, dp, ds, dd):
    gap = 0.05 + 0.025 * p - d
    inverse = lax.rsqrt(s * s + gap * gap + 1e-4)
    dgap = 0.025 * dp - dd
    return ds + dgap - (s * ds + gap * dgap) * inverse


def halves(value):
    high = value.astype(BF16)
    return high, (value - high.astype(F32)).astype(BF16)


def twice(weights, axis):
    return jnp.concatenate([weights, weights], axis=axis)


def split_dot(value, weights, axis):
    return lax.dot_general(
        jnp.concatenate(halves(value), axis=1),
        weights,
        dimension_numbers=(((1,), (axis,)), ((), ())),
        preferred_element_type=F32,
    )


def one_hot(size, index_row):
    shape = (size, index_row.shape[1])
    rows = lax.broadcasted_iota(jnp.int32, shape, 0)
    return jnp.where(rows == index_row, 1.0, 0.0)


class Plan:
    def __init__(self, mesh_shape, pressure, frac, column, cap):
        self.sizes = dict(mesh_shape)
        self.slots = swap_slots(mesh_shape)
        self.z, self.x, self.y = pressure.shape
        self.seg = frac.shape[1]
        self.pairs = column.shape[1]
        self.peers = self.pairs // cap
        self.cap = cap
        self.rows = self.z * self.x
        self.groups = 128 // cap
        self.pack_rows = 6 * self.z // self.groups
        self.half = self.x // 2
        assert self.y == 128 and self.x == self.z == 32
        assert self.groups == 8 and self.peers % self.groups == 0
        self.faces = []
        for axis, _ in self.slots:
            if axis != "gy" or axis not in self.faces:
                self.faces.append(axis)
        self.slot_face = []
        spot = 0
        for i, (axis, _) in enumerate(self.slots):
            if i and not (axis == "gy" and self.slots[i - 1][0] == "gy"):
                spot += 1
            self.slot_face.append(spot)


def plane_rows(plan, z):
    return pl.ds(pl.multiple_of(z * plan.x, 8), plan.x)


def column_masks(plan, column):
    x, y = lax.div(column, plan.y), lax.rem(column, plan.y)
    wide = one_hot(2 * plan.y, lax.div(x, plan.half) * plan.y + y).astype(BF16)
    return wide, one_hot(plan.half, lax.rem(x, plan.half))


STEP = 8


def gather_cells(plan, fields, column, dst):
    wide, one_x = column_masks(plan, column)
    wide = twice(wide, 0)

    def body(c, carry):
        for f, field in enumerate(fields):
            rows = pl.ds(pl.multiple_of(c * STEP * plan.x, 8), STEP * plan.x)
            value = field[rows, :].reshape(STEP, plan.x, plan.y)
            sides = [
                value[:, i * plan.half : (i + 1) * plan.half].reshape(STEP * plan.half, plan.y)
                for i in (0, 1)
            ]
            got = split_dot(jnp.concatenate(sides, axis=1), wide, 0)
            got = got.reshape(STEP, plan.half, plan.pairs) * one_x[None]
            start = pl.multiple_of((3 + f) * plan.z + c * STEP, 8)
            dst[pl.ds(start, STEP), :] = jnp.sum(got, axis=1)
        return carry

    lax.fori_loop(0, plan.z // STEP, body, 0, unroll=2)


def scatter_cells(plan, rates, column, dsts, y_store):
    wide, one_x = column_masks(plan, column)
    lane = lax.broadcasted_iota(jnp.int32, (plan.x, 128), 1)
    edge = (lane == 0) | (lane == 127)
    wide = twice(wide, 1)

    def body(c, carry):
        for f, dst in enumerate(dsts):
            block = rates[pl.ds(pl.multiple_of(f * plan.z + c * STEP, 8), STEP), :]
            spread = jnp.concatenate(
                [one_x * block[j : j + 1, :] for j in range(STEP)], axis=0
            )
            got = split_dot(spread, wide, 1)
            for j in range(STEP):
                z = c * STEP + j
                here = plane_rows(plan, z)
                rows = slice(j * plan.half, (j + 1) * plan.half)
                off = jnp.concatenate(
                    [got[rows, i * plan.y : (i + 1) * plan.y] for i in (0, 1)], axis=0
                )
                if "gy" in plan.faces:
                    turn = lax.rem(255 - 2 * z, 128)
                    off = off - jnp.where(edge, pltpu.roll(y_store[f], turn, 1), 0.0)
                dst[here, :] = dst[here, :] - off
        return carry

    lax.fori_loop(0, plan.z // STEP, body, 0, unroll=2)


def gather_segments(plan, fields, segment, dst):
    one_s = twice(one_hot(plan.seg, segment).astype(BF16), 0)
    for f, field in enumerate(fields):
        dst[f * plan.z : (f + 1) * plan.z, :] = split_dot(field[...], one_s, 0)


def scatter_segments(plan, rate, segment):
    one_s = twice(one_hot(plan.seg, segment).astype(BF16), 1)
    return split_dot(rate, one_s, 1)


def block_transpose(plan, tiles):
    tiles = list(tiles)
    block = lax.broadcasted_iota(jnp.int32, tiles[0].shape, 1) // plan.cap
    bit = 1
    while bit < plan.groups:
        clear = (block & bit) == 0
        for i in range(plan.groups):
            if i & bit:
                continue
            low, high = tiles[i], tiles[i | bit]
            shift = bit * plan.cap
            tiles[i] = jnp.where(clear, low, pltpu.roll(high, shift, 1))
            tiles[i | bit] = jnp.where(clear, pltpu.roll(low, 128 - shift, 1), high)
        bit *= 2
    return tiles


def pack_pairs(plan, own, dst):
    n = plan.pack_rows
    for half in range(plan.pairs // 128):
        lanes = slice(half * 128, (half + 1) * 128)
        tiles = [own[g * n : (g + 1) * n, lanes] for g in range(plan.groups)]
        for c, tile in enumerate(block_transpose(plan, tiles)):
            dst[half * plan.groups + c, 0:n, :] = tile


def unpack_pairs(plan, src, dst):
    n = plan.pack_rows
    for half in range(plan.pairs // 128):
        lanes = slice(half * 128, (half + 1) * 128)
        tiles = [src[half * plan.groups + c, 0:n, :] for c in range(plan.groups)]
        for g, tile in enumerate(block_transpose(plan, tiles)):
            dst[g * n : (g + 1) * n, lanes] = tile


def write_faces(plan, fields, outs):
    pair = lax.broadcasted_iota(jnp.int32, (plan.x, 128), 1) // 2
    y_out = None
    for (axis, odd), spot in zip(plan.slots, plan.slot_face):
        out = outs[spot]
        high, _ = slot_side(axis, odd, plan.sizes)
        if axis == "gx":
            row = jnp.where(high, plan.x - 1, 0)
            for f, field in enumerate(fields):
                out[f] = field[pl.ds(row, plan.z, stride=plan.x), :]
        elif axis == "gz":
            start = pl.multiple_of(jnp.where(high, (plan.z - 1) * plan.x, 0), 8)
            for f, field in enumerate(fields):
                out[f] = field[pl.ds(start, plan.x), :]
        else:
            y_out = out
    if y_out is None:
        return
    zero = jnp.zeros((plan.x, 128), F32)

    def body(c, carry):
        carry = list(carry)
        for j in range(8):
            z = c * 8 + j
            for f, field in enumerate(fields):
                value = field[plane_rows(plan, z), :]
                carry[f] = jnp.where(pair == z, pltpu.roll(value, 2 * z + 1, 1), carry[f])
        return tuple(carry)

    for f, value in enumerate(lax.fori_loop(0, plan.z // 8, body, (zero,) * len(fields))):
        y_out[f] = value


def merge_faces(plan, own, recv, count, gas=0):
    lane = lax.broadcasted_iota(jnp.int32, (plan.x, 128), 1)
    even = lane % 2 == 0
    found = []
    y_recv = []
    for i, (axis, odd) in enumerate(plan.slots):
        high, valid = slot_side(axis, odd, plan.sizes)
        many = count + (gas if axis == "gz" else 0)
        mine = tuple(own[plan.slot_face[i]][f] for f in range(many))
        theirs = tuple(recv[i][f] for f in range(many))
        if axis != "gy":
            found.append((axis, high, valid, mine, theirs))
            continue
        y_recv.append((high, theirs))
        if odd or plan.sizes["gy"] == 2:
            first = y_recv[0][0]
            above = tuple(jnp.where(first, a, b) for a, b in zip(y_recv[0][1], y_recv[-1][1]))
            below = tuple(jnp.where(first, b, a) for a, b in zip(y_recv[0][1], y_recv[-1][1]))
            merged = tuple(
                jnp.where(even, pltpu.roll(a, 127, 1), pltpu.roll(b, 1, 1))
                for a, b in zip(above, below)
            )
            index = lax.axis_index("gy")
            up = jnp.where(index + 1 < plan.sizes["gy"], 1, 0)
            down = jnp.where(index > 0, 1, 0)
            inside = jnp.where(even, up, down) * jnp.where(lane < 2 * plan.z, 1, 0)
            found.append((axis, None, inside == 1, mine, merged))
    return found


def vertical_sign(axis, high):
    if axis != "gz":
        return None
    return jnp.where(high, 1.0, -1.0).astype(F32)


def add_faces(plan, faces, fluxes, dsts, y_store):
    for (axis, high, *_), pair in zip(faces, fluxes):
        for i, (dst, flux) in enumerate(zip(dsts, pair)):
            if axis == "gx":
                rows = pl.ds(jnp.where(high, plan.x - 1, 0), plan.z, stride=plan.x)
                dst[rows, :] = dst[rows, :] + flux
            elif axis == "gz":
                start = pl.multiple_of(jnp.where(high, (plan.z - 1) * plan.x, 0), 8)
                rows = pl.ds(start, plan.x)
                dst[rows, :] = dst[rows, :] + flux
            else:
                y_store[i] = flux


UNROLL = 4


def sweep(plan, plane, dsts, fx, carry, first, count):
    def body(c, carry):
        carry = list(carry)
        for u in range(UNROLL):
            z = first + c * UNROLL + u
            here = plane_rows(plan, z)
            for i, (along_y, along_x, along_z) in enumerate(plane(z)):
                slot = 2 * u + i
                total = dsts[i][here, :] + (along_y - pltpu.roll(along_y, 1, 1))
                fx[slot, 8 : 8 + plan.x, :] = along_x
                total = total + (along_x - fx[slot, 7 : 7 + plan.x, :])
                dsts[i][here, :] = total + (along_z - carry[i])
                carry[i] = along_z
        return tuple(carry)

    return lax.fori_loop(0, count // UNROLL, body, carry)


def sweep_start(plan, fx):
    zero = jnp.zeros((plan.x, 128), F32)
    for i in range(2 * UNROLL):
        fx[i, 0:8, :] = jnp.zeros((8, 128), F32)
    return zero, zero


CHUNKS = 4


def chunk_rows(plan, c):
    size = plan.rows // CHUNKS
    return pl.ds(c * size, size)


def chunk_loop(plan, c, body):
    size = plan.z // CHUNKS
    lax.fori_loop(c * size, (c + 1) * size, body, 0)


def residual_plane(plan, base, k_ref, coef):
    p_ref, w_ref, h_ref, g_ref = base
    lane = lax.broadcasted_iota(jnp.int32, (plan.x, 128), 1)
    row = lax.broadcasted_iota(jnp.int32, (plan.x, 128), 0)
    back = lambda v: pltpu.roll(v, 127, 1)

    def plane(z):
        here, below = plane_rows(plan, z), plane_rows(plan, z + 1)
        beside = pl.ds(z * plan.x + 1, plan.x)
        p0, w0, h0, k0 = (r[here, :] for r in (p_ref, w_ref, h_ref, k_ref))
        flows = []
        sides = (
            (0, lane == 127, tuple(back(v) for v in (p0, w0, h0, k0))),
            (3, row == plan.x - 1, tuple(r[beside, :] for r in (p_ref, w_ref, h_ref, k_ref))),
        )
        for spot, last, (p1, w1, h1, k1) in sides:
            k = jnp.where(last, 0.0, k0 * k1 / (k0 + k1))
            drop, w, h = k * (p0 - p1), w0 + w1, h0 + h1
            coef[spot, here, :] = drop
            coef[spot + 1, here, :] = k * w
            coef[spot + 2, here, :] = k * h
            flows.append((drop * w, drop * h))
        p1, w1, h1, k1 = (r[below, :] for r in (p_ref, w_ref, h_ref, k_ref))
        k = jnp.where(z == plan.z - 1, 0.0, 0.2).astype(F32) * (k0 * k1 / (k0 + k1))
        total = 0.0125 * (p0 + p1)
        drop = k * (p0 - p1 + (0.5 + total))
        extra = k * (total - 0.4)
        w, h, g = w0 + w1, h0 + h1, g_ref[here, :] + g_ref[below, :]
        for i, value in enumerate((drop, k * w, k * h, extra, k * g)):
            coef[6 + i, here, :] = value
        flows.append((drop * w, drop * h + extra * g))
        return tuple(zip(*flows))

    return plane


def jacobian_plane(plan, steps, coef):
    q_ref, a_ref, b_ref, c_ref = steps
    back = lambda v: pltpu.roll(v, 127, 1)

    def plane(z):
        here, below = plane_rows(plan, z), plane_rows(plan, z + 1)
        beside = pl.ds(z * plan.x + 1, plan.x)
        q0, a0, b0 = q_ref[here, :], a_ref[here, :], b_ref[here, :]
        flows = []
        sides = (
            (0, tuple(back(v) for v in (q0, a0, b0))),
            (3, tuple(r[beside, :] for r in (q_ref, a_ref, b_ref))),
        )
        for spot, (q1, a1, b1) in sides:
            drop, w, h = (coef[spot + i, here, :] for i in range(3))
            dq = q0 - q1
            flows.append(((a0 + a1) * drop + w * dq, (b0 + b1) * drop + h * dq))
        q1, a1, b1 = q_ref[below, :], a_ref[below, :], b_ref[below, :]
        drop, w, h, extra, g = (coef[6 + i, here, :] for i in range(5))
        dtotal = 0.0125 * (q0 + q1)
        dq = q0 - q1 + dtotal
        c = c_ref[here, :] + c_ref[below, :]
        flows.append(
            ((a0 + a1) * drop + w * dq, (b0 + b1) * drop + h * dq + (c * extra + g * dtotal))
        )
        return tuple(zip(*flows))

    return plane


class Copies:
    def __init__(self, sems):
        self.sems, self.used = sems, 0

    def start(self, src, dst):
        copy = pltpu.make_async_copy(src, dst, self.sems.at[self.used])
        self.used += 1
        copy.start()
        return copy


def wait_all(copies):
    for copy in copies:
        copy.wait()


class Transfers:
    def __init__(self, sems):
        self.copies = Copies(sems)
        self.loads, self.results, self.stores = {}, {}, []

    def load(self, src, dst):
        self.loads[id(dst)] = self.copies.start(src, dst)

    def result(self, src, dst):
        self.results[id(src)] = (src, dst)

    def ready(self, *refs):
        for ref in refs:
            copy = self.loads.pop(id(ref), None)
            if copy is not None:
                copy.wait()

    def done(self, *refs):
        for ref in refs:
            self.stores.append(self.copies.start(*self.results.pop(id(ref))))

    def finish(self):
        wait_all(list(self.loads.values()))
        for src, dst in self.results.values():
            self.stores.append(self.copies.start(src, dst))
        wait_all(self.stores)


def clear_tails(plan, refs):
    for ref in refs:
        ref[plan.rows : plan.rows + plan.x + 8, :] = jnp.zeros((plan.x + 8, 128), F32)


def face_base(sign, conductance, own, other, coef):
    (w0, h0, g0), (w1, h1, g1) = mobilities(*own), mobilities(*other)
    p0, p1 = own[0], other[0]
    water, hydrogen = w0 + w1, h0 + h1
    drop = p0 - p1
    if sign is not None:
        total = 0.0125 * (p0 + p1)
        drop = drop + sign * (0.5 + total)
    drop = conductance * drop
    coef[0], coef[1], coef[2] = drop, conductance * water, conductance * hydrogen
    if sign is None:
        coef[3] = jnp.zeros(drop.shape, F32)
        coef[4] = jnp.zeros(drop.shape, F32)
        return drop * water, drop * hydrogen
    extra = conductance * (sign * (total - 0.4))
    coef[3], coef[4] = extra, conductance * (g0 + g1)
    return drop * water, drop * hydrogen + extra * (g0 + g1)


def face_step(sign, coef, own, other):
    q0, q1 = own[0], other[0]
    water, hydrogen = own[1] + other[1], own[2] + other[2]
    dq = q0 - q1
    if sign is not None:
        dtotal = sign * (0.0125 * (q0 + q1))
        dq = dq + dtotal
    out_w = water * coef[0] + coef[1] * dq
    out_h = hydrogen * coef[0] + coef[2] * dq
    if sign is not None:
        out_h = out_h + (own[3] + other[3]) * coef[3] + coef[4] * dtotal
    return out_w, out_h


def moves_of(p, s, d, dp, ds, dd):
    return mobility_moves(1.0 + 0.05 * p, 2.0 + p, 1.0 - s, s, d, dp, ds, dd)[:3]


def first_kernel(plan, io, *refs):
    n = len(plan.faces)
    grids = refs[:4]
    fp, fs, fd, segment, column, kind, count, table = refs[4:12]
    faces, (pack, own, weight) = refs[12 : 12 + n], refs[12 + n : 15 + n]
    local, sems = refs[15 + n :]
    copies = Copies(sems)
    loads = [copies.start(g, local.at[i]) for i, g in enumerate(grids)]
    io.ready(fp, fs, fd, segment, kind, column)
    gather_segments(plan, (fp, fs, fd), segment[...], own)
    kinds = kind[...]
    picked = jnp.zeros(kinds.shape, F32)
    for j in range(table.shape[0]):
        picked = jnp.where(kinds == j, table[j], picked)
    slot = lax.broadcasted_iota(jnp.int32, kinds.shape, 1)
    block, rank = slot // plan.cap, lax.rem(slot, plan.cap)
    live = jnp.zeros(kinds.shape, jnp.int32)
    for j in range(plan.peers):
        live = jnp.where(block == j, count[0, j], live)
    picked = jnp.where(rank < live, picked, 0.0)
    weight[...] = picked
    for half in range(plan.pairs // 128):
        tile = jnp.broadcast_to(picked[:, half * 128 : (half + 1) * 128], (8, 128))
        for c in range(plan.groups):
            moved = pltpu.roll(tile, 128 - c * plan.cap, 1) if c else tile
            pack[half * plan.groups + c, plan.pack_rows : plan.pack_rows + 8, :] = moved
    wait_all(loads[:3])
    fields = tuple(local.at[i] for i in range(4))
    gather_cells(plan, fields[:3], column[...], own)
    pack_pairs(plan, own, pack)
    io.done(own, pack, weight)
    wait_all(loads[3:])
    write_faces(plan, fields, faces)


def pair_values(plan, ref, side):
    first = 3 * side
    return tuple(ref[(first + f) * plan.z : (first + f + 1) * plan.z, :] for f in range(3))


def residual_inner(plan, io, *refs):
    grids, (_, res_out, coef_out) = refs[:7], refs[7:10]
    sp, sk, sw, sh, sg, local, res, coef, fx, sems = refs[10:]
    copies = Copies(sems)
    places = [sp] + [local.at[i] for i in range(5)] + [sk]
    loads = [
        [
            copies.start(grid.at[chunk_rows(plan, c)], place.at[chunk_rows(plan, c)])
            for grid, place in zip(grids, places)
        ]
        for c in range(CHUNKS)
    ]
    s, d, old_water, old_hydrogen, volume = (local.at[i] for i in range(5))
    res_w, res_h, res_c = (res.at[i] for i in range(3))
    clear_tails(plan, (sp, sw, sh, sg))
    sk[plan.rows : plan.rows + plan.x + 8, :] = jnp.ones((plan.x + 8, 128), F32)

    def cells(z, carry):
        here = plane_rows(plan, z)
        pv, sv, dv = sp[here, :], s[here, :], d[here, :]
        sw[here, :], sh[here, :], sg[here, :] = mobilities(pv, sv, dv)
        mw, mh = masses(pv, sv, dv)
        vol = volume[here, :]
        res_w[here, :] = vol * (mw - old_water[here, :])
        res_h[here, :] = vol * (mh - old_hydrogen[here, :])
        res_c[here, :] = closure(pv, sv, dv)
        return carry

    for c in range(CHUNKS):
        wait_all(loads[c])
        chunk_loop(plan, c, cells)
    plane = residual_plane(plan, (sp, sw, sh, sg), sk, coef)
    carry = sweep_start(plan, fx)
    stores = []
    for c in range(CHUNKS):
        size = plan.z // CHUNKS
        carry = sweep(plan, plane, (res_w, res_h), fx, carry, c * size, size)
        rows = chunk_rows(plan, c)
        stores.append(copies.start(res.at[:, rows], res_out.at[:, rows]))
        stores.append(copies.start(coef.at[:, rows], coef_out.at[:, rows]))
    wait_all(stores)


def residual_kernel(plan, io, *refs):
    n, m = len(plan.slots), len(plan.faces)
    refs = list(refs)
    take = lambda count: [refs.pop(0) for _ in range(count)]
    (res_in,) = take(1)
    fp, fs, fd, frac_water, frac_hydrogen, frac_volume = take(6)
    segment, column, weight, own, recv = take(5)
    own_faces, recv_faces = take(m), take(n)
    res_out, frac_res, face_coef = take(3)
    faces = take(m)
    pack, own_res, pair_coef = take(3)
    res, y_store, rates, sems, got, weight_back = take(6)
    fields = tuple(res.at[i] for i in range(3))
    copies = Copies(sems)
    load = copies.start(res_in, res)

    io.ready(recv)
    unpack_pairs(plan, recv, got)
    lane8 = lax.broadcasted_iota(jnp.int32, (8, 128), 1) // plan.cap
    for half in range(plan.pairs // 128):
        total = None
        for c in range(plan.groups):
            tile = recv[half * plan.groups + c, plan.pack_rows : plan.pack_rows + 8, :]
            moved = pltpu.roll(tile, c * plan.cap, 1) if c else tile
            total = moved if total is None else jnp.where(lane8 == c, moved, total)
        weight_back[:, half * 128 : (half + 1) * 128] = total[0:1, :]
    io.ready(own, weight, segment, column, fp, fs, fd)
    io.ready(frac_water, frac_hydrogen, frac_volume)

    def pair_rates(side, weights, seg_values, cell_values):
        w0, h0, _ = mobilities(*seg_values)
        w1, h1, _ = mobilities(*cell_values)
        half = 0.5 * weights
        flow = half * (seg_values[0] - cell_values[0])
        water, hydrogen = w0 + w1, h0 + h1
        for j, value in enumerate((flow, half * water, half * hydrogen)):
            start = (3 * side + j) * plan.z
            pair_coef[start : start + plan.z, :] = value
        return flow * water, flow * hydrogen

    rate_w, rate_h = pair_rates(
        1, weight_back[...], pair_values(plan, own, 0), pair_values(plan, got, 1)
    )
    fpv, fsv, fdv = fp[...], fs[...], fd[...]
    mass_w, mass_h = masses(fpv, fsv, fdv)
    vol = frac_volume[...]
    frac_res[0] = vol * (mass_w - frac_water[...]) + scatter_segments(plan, rate_w, segment[...])
    frac_res[1] = vol * (mass_h - frac_hydrogen[...]) + scatter_segments(
        plan, rate_h, segment[...]
    )
    frac_res[2] = closure(fpv, fsv, fdv)
    io.done(frac_res)
    rate_w, rate_h = pair_rates(
        0, weight[...], pair_values(plan, got, 0), pair_values(plan, own, 1)
    )
    io.done(pair_coef)
    rates[0 : plan.z, :] = rate_w
    rates[plan.z : 2 * plan.z, :] = rate_h

    io.ready(*own_faces, *recv_faces)
    found = merge_faces(plan, own_faces, recv_faces, 4)
    fluxes = []
    for i, (axis, high, valid, mine, theirs) in enumerate(found):
        k0, k1 = mine[3], theirs[3]
        scale = 0.2 if axis == "gz" else 1.0
        conductance = jnp.where(
            valid, scale * (k0 * k1 / jnp.where(valid, k0 + k1, 1.0)), 0.0
        )
        sign = vertical_sign(axis, high)
        fluxes.append(face_base(sign, conductance, mine[:3], theirs[:3], face_coef.at[i]))
    io.done(face_coef)
    load.wait()
    add_faces(plan, found, fluxes, fields[:2], y_store)
    scatter_cells(plan, rates, column[...], fields[:2], y_store)
    store = copies.start(res, res_out)
    send_parts(plan, io, fields, frac_res, segment, column, faces, own_res, pack, own, own_faces)
    store.wait()


def send_parts(
    plan, io, fields, frac_fields, segment, column, faces, own, pack, base_own, base_faces
):
    gather_segments(plan, tuple(frac_fields.at[i] for i in range(3)), segment[...], own)
    gather_cells(plan, fields, column[...], own)
    for side in (0, 1):
        moves = moves_of(*pair_values(plan, base_own, side), *pair_values(plan, own, side))
        for j in (0, 1):
            start = (3 * side + 1 + j) * plan.z
            own[start : start + plan.z, :] = moves[j]
    pack_pairs(plan, own, pack)
    io.done(own, pack)
    write_faces(plan, fields, faces)
    for axis, face, base in zip(plan.faces, faces, base_faces):
        three = lambda ref: tuple(ref[f] for f in range(3))
        moves = moves_of(*three(base), *three(face))
        for j in range(3 if axis == "gz" else 2):
            face[1 + j] = moves[j]
        io.done(face)


def total_of(value):
    return jnp.sum(jnp.sum(value, axis=0, keepdims=True), axis=1, keepdims=True)


def block_sums(plan, cell_refs, frac_refs, function, count):
    def body(z, carry):
        here = plane_rows(plan, z)
        for f in range(3):
            parts = function(*(group[f][here, :] for group in cell_refs))
            carry = tuple(c + part for c, part in zip(carry, parts))
        return carry

    zero = jnp.zeros((plan.x, 128), F32)
    sums = lax.fori_loop(0, plan.z, body, (zero,) * count, unroll=2)
    sums = [total_of(v) for v in sums]
    for f in range(3):
        parts = function(*(ref[f] for ref in frac_refs))
        sums = [v + total_of(part) for v, part in zip(sums, parts)]
    return sums


def safe_ratio(top, bottom):
    good = bottom > 0.0
    return jnp.where(good, top / jnp.where(good, bottom, 1.0), 0.0)


def jacobian_inner(plan, last, io, *refs):
    refs = list(refs)
    take = lambda count: [refs.pop(0) for _ in range(count)]
    grids = take(4)
    vec_in, coef_in = take(2)
    if last:
        base_in, base_frac, frac_vec = take(3)
        out_back, stats = take(2)
    else:
        (out_back,) = take(1)
    sq, sa, sb, sc, local, coef, out, fx, sems = take(9)
    copies = Copies(sems)
    places = [sq] + [local.at[i] for i in range(6)]
    sources = [vec_in.at[i] for i in range(3)] + list(grids)
    loads = [
        [
            copies.start(grid.at[chunk_rows(plan, c)], place.at[chunk_rows(plan, c)])
            for grid, place in zip(sources, places)
        ]
        for c in range(CHUNKS)
    ]
    coefs = [
        copies.start(coef_in.at[:, chunk_rows(plan, c)], coef.at[:, chunk_rows(plan, c)])
        for c in range(CHUNKS)
    ]
    if last:
        (base,) = take(1)
        late = copies.start(base_in, base)
    v1, v2, p, s, d, volume = (local.at[i] for i in range(6))
    out_w, out_h, out_c = (out.at[i] for i in range(3))
    clear_tails(plan, (sq, sa, sb, sc))

    def cells(z, carry):
        here = plane_rows(plan, z)
        values = tuple(r[here, :] for r in (p, s, d, sq, v1, v2))
        sa[here, :], sb[here, :], sc[here, :], mw, mh, out_c[here, :] = cell_steps(*values)
        vol = volume[here, :]
        out_w[here, :] = vol * mw
        out_h[here, :] = vol * mh
        return carry

    for c in range(CHUNKS):
        wait_all(loads[c])
        chunk_loop(plan, c, cells)
    plane = jacobian_plane(plan, (sq, sa, sb, sc), coef)
    carry = sweep_start(plan, fx)
    stores = []
    for c in range(CHUNKS):
        coefs[c].wait()
        size = plan.z // CHUNKS
        carry = sweep(plan, plane, (out_w, out_h), fx, carry, c * size, size)
        rows = chunk_rows(plan, c)
        stores.append(copies.start(out.at[:, rows], out_back.at[:, rows]))
    if last:
        late.wait()
        io.ready(base_frac, frac_vec)
        groups = (tuple(base.at[i] for i in range(3)), (sq, v1, v2))
        fracs = (base_frac, frac_vec)
        rr, rw = block_sums(plan, groups, fracs, lambda r, w: (r * r, r * w), 2)
        share = safe_ratio(rw, rr)
        (uu,) = block_sums(plan, groups, fracs, lambda r, w: (jnp.square(w - share * r),), 1)
        r11 = jnp.sqrt(rr)
        put_lanes(stats, (r11, safe_ratio(rw, r11), jnp.sqrt(uu), share, uu))
    wait_all(stores)


def put_lanes(out, values):
    lane = lax.broadcasted_iota(jnp.int32, out.shape, 1)
    total = jnp.zeros(out.shape, F32)
    for j, value in enumerate(values):
        total = jnp.where(lane == j, value, total)
    out[...] = total


def jacobian_kernel(plan, last, io, *refs):
    n, m = len(plan.slots), len(plan.faces)
    refs = list(refs)
    take = lambda count: [refs.pop(0) for _ in range(count)]
    out_in, face_coef, pair_coef = take(3)
    fp, fs, fd, frac_volume, frac_vec = take(5)
    segment, column, own_vec, recv = take(4)
    own_vec_faces, recv_vec_faces = take(m), take(n)
    if last:
        vec_in, base_in, base_frac, stats_in = take(4)
        (stats,) = take(1)
    else:
        (own,) = take(1)
        own_faces = take(m)
        out_back, frac_out = take(2)
        faces = take(m)
        pack, own_out = take(2)
    out, y_store, rates, sems, got_vec = take(5)
    fields = tuple(out.at[i] for i in range(3))
    copies = Copies(sems)
    load = copies.start(out_in, out)
    if last:
        vec, base, frac_out = take(3)
        late = [copies.start(vec_in, vec), copies.start(base_in, base)]

    io.ready(recv)
    unpack_pairs(plan, recv, got_vec)
    io.ready(own_vec, pair_coef, segment, column)
    io.ready(fp, fs, fd, frac_volume, frac_vec)

    def pair_rates(side, seg_steps, cell_steps):
        flow, water, hydrogen = pair_values(plan, pair_coef, side)
        q, a, b = (f(x, y) for f, x, y in zip((lax.sub, lax.add, lax.add), seg_steps, cell_steps))
        return a * flow + water * q, b * flow + hydrogen * q

    rate_w, rate_h = pair_rates(1, pair_values(plan, own_vec, 0), pair_values(plan, got_vec, 1))
    values = (fp[...], fs[...], fd[...], frac_vec[0], frac_vec[1], frac_vec[2])
    _, _, _, mass_w, mass_h, frac_out[2] = cell_steps(*values)
    vol = frac_volume[...]
    frac_out[0] = vol * mass_w + scatter_segments(plan, rate_w, segment[...])
    frac_out[1] = vol * mass_h + scatter_segments(plan, rate_h, segment[...])
    if not last:
        io.done(frac_out)
    rate_w, rate_h = pair_rates(0, pair_values(plan, got_vec, 0), pair_values(plan, own_vec, 1))
    rates[0 : plan.z, :] = rate_w
    rates[plan.z : 2 * plan.z, :] = rate_h

    io.ready(*own_vec_faces, *recv_vec_faces, face_coef)
    found = merge_faces(plan, own_vec_faces, recv_vec_faces, 3, gas=1)
    fluxes = [
        face_step(vertical_sign(axis, high), face_coef.at[i], mine, theirs)
        for i, (axis, high, _, mine, theirs) in enumerate(found)
    ]
    load.wait()
    add_faces(plan, found, fluxes, fields[:2], y_store)
    scatter_cells(plan, rates, column[...], fields[:2], y_store)
    if not last:
        store = copies.start(out, out_back)
        io.ready(own, *own_faces)
        send_parts(
            plan, io, fields, frac_out, segment, column, faces, own_out, pack, own, own_faces
        )
        store.wait()
        return
    wait_all(late)
    io.ready(base_frac, stats_in)
    known = stats_in[0:1, :]
    lane1 = lax.broadcasted_iota(jnp.int32, (1, 128), 1)
    r11, r12, r22, share, uu = (
        jnp.sum(jnp.where(lane1 == j, known, 0.0), axis=1, keepdims=True) for j in range(5)
    )
    three = lambda ref: tuple(ref.at[i] for i in range(3))
    refs3 = (three(base), three(vec), fields)
    fracs3 = (base_frac, frac_vec, frac_out)
    rz, wz = block_sums(
        plan, refs3, fracs3, lambda r, w, v: (r * v, w * v), 2
    )
    uz = wz - share * rz
    along_r, along_u = safe_ratio(rz, r11 * r11), safe_ratio(uz, uu)
    rest = along_r - along_u * share
    (vv,) = block_sums(
        plan,
        refs3,
        fracs3,
        lambda r, w, v: (jnp.square((v - rest * r) - along_u * w),),
        1,
    )
    put_lanes(stats, (r11, r12, r22, safe_ratio(rz, r11), safe_ratio(uz, r22), jnp.sqrt(vv)))


def step_kernel(plan, io, stats, res_in, frac_res, vec_in, frac_vec, out, frac_step, *scratch):
    res, vec, step, sems = scratch
    copies = Copies(sems)
    loads = [
        [copies.start(a.at[f], b.at[f]) for a, b in ((res_in, res), (vec_in, vec))]
        for f in range(3)
    ]
    io.ready(stats)
    table = stats[...]
    lane = lax.broadcasted_iota(jnp.int32, table.shape, 1)
    r11, r12, r22, r13, r23, r33 = (
        jnp.sum(jnp.where(lane == j, table, 0.0), axis=1, keepdims=True) for j in range(6)
    )
    add = lambda v: jnp.sum(v, axis=0, keepdims=True)
    norm2 = add(r11 * r11) + EPS
    norm = jnp.sqrt(norm2)
    c11 = add(r11 * r12) / norm2
    left1, left2 = r12 - c11 * r11, r22
    c21 = jnp.sqrt(add(left1 * left1 + left2 * left2) / norm2 + EPS)
    scale = 1.0 / (norm * c21)
    second1, second2 = -scale * left1, -scale * left2
    image1 = -scale * (r13 - c11 * r12)
    image2 = -scale * (r23 - c11 * r22)
    image3 = -scale * r33
    first1 = -r11 / norm
    c12 = add(image1 * first1)
    c22 = add(image1 * second1 + image2 * second2)
    u1 = image1 - c12 * first1 - c22 * second1
    u2 = image2 - c22 * second2
    c32_2 = add(u1 * u1 + u2 * u2 + image3 * image3) + EPS
    rho = jnp.sqrt(c11 * c11 + c21 * c21)
    co, si = c11 / rho, c21 / rho
    t1 = co * c12 + si * c22
    t2 = co * c22 - si * c12
    y2 = -si * norm * t2 / (t2 * t2 + c32_2)
    y1 = (co * norm - t1 * y2) / rho
    on_vec = -y2 * scale
    on_res = -y1 / norm - c11 * on_vec
    stores = []
    for f in range(3):
        wait_all(loads[f])

        def body(z, carry):
            here = plane_rows(plan, z)
            step[f, here, :] = on_res * res[f, here, :] + on_vec * vec[f, here, :]
            return carry

        lax.fori_loop(0, plan.z, body, 0, unroll=4)
        stores.append(copies.start(step.at[f], out.at[f]))
    io.ready(frac_res, frac_vec)
    for f in range(3):
        frac_step[f] = on_res * frac_res[f] + on_vec * frac_vec[f]
    wait_all(stores)


def call(
    kernel,
    out_shapes,
    args,
    scratch,
    copies,
    more=(),
    smem=(),
    far=(),
    far_out=(),
    first=(),
    work=0,
):
    place = lambda i: pltpu.SMEM if i in smem else pl.ANY
    cost = pl.CostEstimate(flops=work, bytes_accessed=work, transcendentals=0) if work else None
    near = [i for i in first + tuple(range(len(args))) if i not in smem and i not in far]
    near = list(dict.fromkeys(near))
    near_out = [i for i in range(len(out_shapes)) if i not in far_out]

    def body(*refs):
        refs = list(refs)
        take = lambda count: [refs.pop(0) for _ in range(count)]
        ins, outs = take(len(args)), take(len(out_shapes))
        own = take(len(scratch) + 1 + len(more))
        io = Transfers(refs[-1])
        for i in near:
            buffer = refs.pop(0)
            io.load(ins[i], buffer)
            ins[i] = buffer
        for i in near_out:
            buffer = refs.pop(0)
            io.result(buffer, outs[i])
            outs[i] = buffer
        kernel(io, *ins, *outs, *own)
        io.finish()

    return pl.pallas_call(
        body,
        out_shape=[jax.ShapeDtypeStruct(shape, F32) for shape in out_shapes],
        in_specs=[pl.BlockSpec(memory_space=place(i)) for i in range(len(args))],
        out_specs=[pl.BlockSpec(memory_space=pl.ANY)] * len(out_shapes),
        scratch_shapes=[pltpu.VMEM(shape, F32) for shape in scratch]
        + [pltpu.SemaphoreType.DMA((copies,))]
        + [pltpu.VMEM(shape, F32) for shape in more]
        + [pltpu.VMEM(args[i].shape, args[i].dtype) for i in near]
        + [pltpu.VMEM(out_shapes[i], F32) for i in near_out]
        + [pltpu.SemaphoreType.DMA((len(near) + len(near_out) + 1,))],
        compiler_params=pltpu.CompilerParams(vmem_limit_bytes=VMEM_BYTES),
        cost_estimate=cost,
    )(*args)


def on_device(mesh_shape, *args):
    (
        pressure,
        saturation,
        dissolved,
        old_water,
        old_hydrogen,
        pore_volume,
        permeability,
        frac_pressure,
        frac_saturation,
        frac_dissolved,
        frac_old_water,
        frac_old_hydrogen,
        frac_volume,
        pair_segment,
        pair_column,
        pair_kind,
        pair_count,
        transfer_table,
    ) = args
    cap = pair_column.shape[1] // pair_count.shape[1]
    plan = Plan(mesh_shape, pressure, frac_pressure, pair_column, cap)
    slots = len(plan.slots)
    devices = plan.sizes["gx"] * plan.sizes["gy"] * plan.sizes["gz"]
    flat = lambda a: a.reshape(plan.rows, plan.y)
    p, s, d, k = (flat(a) for a in (pressure, saturation, dissolved, permeability))
    volume = flat(pore_volume)
    field = (plan.rows, plan.y)
    padded = (plan.rows + plan.x + 8, plan.y)
    pair_shape = (6 * plan.z, plan.pairs)
    face_count = len(plan.faces)
    sweep_scratch = (2 * UNROLL, plan.x + 8, plan.y)
    y_scratch = (2, plan.x, plan.y)
    rate_scratch = (2 * plan.z, plan.pairs)
    coef_shape = (11,) + field
    three = (3,) + field
    frac_shape = (3, plan.z, plan.seg)
    inner_work = 16 << 20
    step_faces = [(4 if axis == "gz" else 3, 32, 128) for axis in plan.faces]

    def exchange(faces, pack):
        got = lax.all_to_all(pack, PLANE, 0, 0, tiled=True)
        moved = [
            lax.ppermute(faces[spot], DEVICES, swap_pairs(plan.sizes, axis, odd))
            for (axis, odd), spot in zip(plan.slots, plan.slot_face)
        ]
        return moved, got

    outs = call(
        functools.partial(first_kernel, plan),
        [(4, 32, 128)] * face_count
        + [(plan.peers, plan.pack_rows + 8, 128), pair_shape, (1, plan.pairs)],
        [p, s, d, k, frac_pressure, frac_saturation, frac_dissolved]
        + [pair_segment, pair_column, pair_kind, pair_count, transfer_table],
        scratch=[(4,) + field],
        copies=4,
        smem=(10, 11),
        far=(0, 1, 2, 3),
    )
    faces, (pack, own, weight) = outs[:face_count], outs[face_count:]
    recv_faces, recv = exchange(faces, pack)
    res, coef = call(
        functools.partial(residual_inner, plan),
        [three, coef_shape],
        [p, s, d, flat(old_water), flat(old_hydrogen), volume, k, weight],
        scratch=[padded] * 5 + [(5,) + field, three, coef_shape, sweep_scratch],
        copies=9 * CHUNKS,
        far=range(7),
        far_out=(0, 1),
        work=inner_work,
    )
    outs = call(
        functools.partial(residual_kernel, plan),
        [three, frac_shape, (face_count, 5, 32, 128)]
        + step_faces
        + [(plan.peers, plan.pack_rows, 128), pair_shape, pair_shape],
        [res, frac_pressure, frac_saturation, frac_dissolved]
        + [frac_old_water, frac_old_hydrogen, frac_volume]
        + [pair_segment, pair_column, weight, own, recv]
        + list(faces)
        + list(recv_faces),
        scratch=[three, y_scratch, rate_scratch],
        more=[pair_shape, (1, plan.pairs)],
        copies=2,
        far=(0,),
        far_out=(0,),
        first=(11, 10, 9),
    )
    res, frac_res, face_coef = outs[:3]
    vec_faces = outs[3 : 3 + face_count]
    pack, own_vec, pair_coef = outs[3 + face_count :]

    def image(vec, frac_vec, vec_faces, pack, own_vec, base):
        recv_vec_faces, recv_vec = exchange(vec_faces, pack)
        last = base is not None
        outs = call(
            functools.partial(jacobian_inner, plan, last),
            [three] + ([(8, 128)] if last else []),
            [p, s, d, volume, vec, coef] + ([*base, frac_vec] if last else []),
            scratch=[padded] * 4 + [(6,) + field, coef_shape, three, sweep_scratch],
            more=[three] if last else [],
            copies=9 * CHUNKS + 1,
            far=range(7 if last else 6),
            far_out=(0,),
            work=inner_work,
        )
        args = [outs[0], face_coef, pair_coef]
        args += [frac_pressure, frac_saturation, frac_dissolved, frac_volume, frac_vec]
        args += [pair_segment, pair_column, own_vec, recv_vec]
        args += list(vec_faces) + list(recv_vec_faces)
        if last:
            far = (0, len(args), len(args) + 1)
            args += [vec, *base, outs[1]]
            shapes = [(devices, 8)]
        else:
            far = (0,)
            args += [own] + list(faces)
            shapes = [three, frac_shape] + step_faces
            shapes += [(plan.peers, plan.pack_rows, 128), pair_shape]
        return call(
            functools.partial(jacobian_kernel, plan, last),
            shapes,
            args,
            scratch=[three, y_scratch, rate_scratch],
            more=[pair_shape] + ([three, three, frac_shape] if last else []),
            copies=3,
            far=far,
            far_out=() if last else (0,),
            first=(11, 2, 10),
        )

    outs = image(res, frac_res, vec_faces, pack, own_vec, None)
    vec, frac_vec = outs[:2]
    vec_faces = outs[2 : 2 + face_count]
    pack, own_vec = outs[2 + face_count :]
    (stats,) = image(vec, frac_vec, vec_faces, pack, own_vec, (res, frac_res))
    stats = lax.all_to_all(stats, ("gx", "gy", "gz"), 0, 0, tiled=True)
    step, frac_step = call(
        functools.partial(step_kernel, plan),
        [three, frac_shape],
        [stats, res, frac_res, vec, frac_vec],
        scratch=[three] * 3,
        copies=9,
        far=(1, 3),
        far_out=(0,),
    )
    shape = (3, plan.z, plan.x, plan.y)
    return step.reshape(shape), frac_step, res.reshape(shape), frac_res


def solution(mesh):
    grid = P("gz", "gx", "gy")
    segments = P("gz", PLANE)
    lists = P(PLANE, None)
    return jax.shard_map(
        functools.partial(on_device, dict(mesh.shape)),
        mesh=mesh,
        in_specs=(grid,) * 7 + (segments,) * 6 + (lists,) * 4 + (P(),),
        out_specs=(
            P(None, "gz", "gx", "gy"),
            P(None, "gz", PLANE),
            P(None, "gz", "gx", "gy"),
            P(None, "gz", PLANE),
        ),
        check_vma=False,
    )
```
